256 devices in a mesh: freq: 64 (over y, z, core), sky: 4 (over x).
Axes of the slice: x: 4, y: 4, z: 8, core: 2. Of those that a mesh axis runs over, the one named last changes fastest.
Arguments:
- sky_maps: bfloat16 [1024, 96, 4096], P('freq', 'sky'), may hold values from -240 to 240
- beam_index: int32 [1024], P('freq'), may hold values from 0 to 7
- beam_taps: float32 [8, 31], replicated, may hold values from 0.05 to 1
- start_seed: int32 [1024, 16], replicated, may hold values from -64 to 64
Outputs:
- cleaned: bfloat16 [1024, 256, 1536], P(None, ('freq', 'sky'))
The draws below stay inside these ranges and needn't reach their ends.
All inputs are finite; a program needn't handle non-finite values.
Results may differ from the reference program's by a relative error of at most 0.0079.
The reference program's roundings to bfloat16 on the way (of `smoothed` and `tiled`) count: a program that leaves them out, or rounds other values in their place, can miss the bound.
Values may be sent and summed in bfloat16 or wider, within the bound.
No kernel may reach another device: no remote copies, remote signals or barrier semaphores. Data moves between devices by JAX's collectives and lax.ppermute only.
A program may use at most 64 MiB of HBM per device.

```python
import math
import jax
import jax.numpy as jnp
from jax import lax

C = 1024
TAPS = 31
NB = 8
MODES = 16
ITERS = 8
HD = 24
TW = 64
H = 96
W = 4096
N_FREQ = 64
N_SKY = 4


def draw_sky_maps(key, part):
    components = 24
    base_key = jax.random.fold_in(key, 7)
    key_spec, key_pick, key_amp, key_noise = jax.random.split(base_key, 4)
    spectra = jax.random.normal(key_spec, (components, C), jnp.float32)
    strength = 3.0 * 0.93 ** jnp.arange(components, dtype=jnp.float32)
    chosen = jax.random.randint(key_pick, (H, W), 0, components)
    amplitude = jax.random.normal(key_amp, (H, W), jnp.float32)
    weight = amplitude * strength[chosen]

    def one_block(block_index):
        first_chan = block_index * 16
        local_spec = lax.dynamic_slice_in_dim(spectra, first_chan, 16, 1)
        foreground = jnp.moveaxis(jnp.take(local_spec, chosen, axis=0), 2, 0) * weight[None]
        noise_key = jax.random.fold_in(key_noise, block_index)
        noise_part = jax.random.normal(noise_key, (16, H, W), jnp.float32)
        return jnp.clip(8.0 * (noise_part + foreground), -240.0, 240.0).astype(jnp.bfloat16)
    stacked = lax.map(one_block, jnp.arange(C // 16, dtype=jnp.int32))
    return stacked.reshape(C, H, W)


def place_ends(entries, rng, low, top_value):
    shape = entries.shape
    index_at = [jax.random.randint(jax.random.fold_in(rng, axis), (), 0, shape[axis]) for axis in range(len(shape))]
    entries = entries.at[tuple(index_at)].set(low)
    longest = shape.index(max(shape))
    index_at[longest] = (index_at[longest] + 1) % shape[longest]
    return entries.at[tuple(index_at)].set(top_value)


def setup_inputs(seed: int = 0) -> dict:
    arg_keys = jax.random.split(jax.random.key(seed), 5)
    sky_maps = draw_sky_maps(jax.random.fold_in(arg_keys[4], 71), 0)
    beam_index = place_ends(jax.random.randint(arg_keys[1], (C,), 0, NB), jax.random.fold_in(arg_keys[1], 1), 0, NB - 1).astype(jnp.int32)
    beam_taps = jnp.clip(jnp.exp(jax.random.uniform(arg_keys[2], (NB, TAPS), jnp.float32, math.log(0.05), math.log(1.0))), 0.05, 1.0)
    start_seed = place_ends(jax.random.randint(arg_keys[3], (C, MODES), -64, 65), jax.random.fold_in(arg_keys[3], 1), -64, 64).astype(jnp.int32)
    return dict(sky_maps=sky_maps, beam_index=beam_index, beam_taps=beam_taps, start_seed=start_seed)


def smooth_channels(block, kernels):
    half_taps = (TAPS - 1) // 2
    height = block.shape[1]
    columns = block.shape[2]
    padded = jnp.pad(block, ((0, 0), (half_taps, half_taps), (0, 0)))
    row_pass = jnp.zeros(block.shape, jnp.float32)
    for offset in range(TAPS):
        row_pass = row_pass + kernels[:, offset, None, None] * padded[:, offset:offset + height, :].astype(jnp.float32)
    widened = jnp.pad(row_pass, ((0, 0), (0, 0), (half_taps, half_taps)))
    col_pass = jnp.zeros(block.shape, jnp.float32)
    for offset in range(TAPS):
        col_pass = col_pass + kernels[:, offset, None, None] * widened[:, :, offset:offset + columns]
    return col_pass.astype(jnp.bfloat16)

def reference(sky_maps, beam_index, beam_taps, start_seed):
    chosen = beam_taps[beam_index]
    kernels = chosen / jnp.sum(chosen, axis=1, keepdims=True)
    groups = C // 16
    smoothed = lax.map(lambda pair: smooth_channels(pair[0], pair[1]), (sky_maps.reshape(groups, 16, H, W), kernels.reshape(groups, 16, TAPS)))
    tiled = smoothed.reshape(C, N_SKY, HD, N_FREQ, TW).transpose(0, 3, 1, 2, 4).reshape(C, N_FREQ * N_SKY, HD * TW)

    def add_tile(tile_index, summed):
        tile_data = lax.dynamic_index_in_dim(tiled, tile_index, 1, keepdims=False).astype(jnp.float32)
        return summed + jnp.dot(tile_data, tile_data.T, precision=lax.Precision.HIGHEST)
    covariance = lax.fori_loop(0, N_FREQ * N_SKY, add_tile, jnp.zeros((C, C), jnp.float32)) / (H * W)
    subspace = start_seed.astype(jnp.float32)
    for sweep in range(ITERS):
        images = jnp.dot(covariance, subspace, precision=lax.Precision.HIGHEST)
        gram_matrix = jnp.dot(images.T, images, precision=lax.Precision.HIGHEST)
        factor = jnp.linalg.cholesky(gram_matrix)
        subspace = lax.linalg.triangular_solve(factor, images, left_side=False, lower=True, transpose_a=True)

    def clean_tile(tile_index, result):
        tile_data = lax.dynamic_index_in_dim(tiled, tile_index, 1, keepdims=False).astype(jnp.float32)
        coeffs = jnp.dot(subspace.T, tile_data, precision=lax.Precision.HIGHEST)
        fixed_tile = (tile_data - jnp.dot(subspace, coeffs, precision=lax.Precision.HIGHEST)).astype(jnp.bfloat16)
        return lax.dynamic_update_index_in_dim(result, fixed_tile, tile_index, 1)
    return lax.fori_loop(0, N_FREQ * N_SKY, clean_tile, jnp.zeros((C, N_FREQ * N_SKY, HD * TW), jnp.bfloat16))
```

```python
import jax
import jax.numpy as jnp
from jax import lax
from jax.experimental import pallas as pl
from jax.experimental.pallas import tpu as pltpu
from jax.sharding import Mesh, PartitionSpec as P

ITERS = 8
F32 = jnp.float32
BF16 = jnp.bfloat16
NT = (((1,), (1,)), ((), ()))
TN = (((0,), (0,)), ((), ()))
VMEM_LIMIT = 60 * 1024 * 1024


def vmem():
    return pl.BlockSpec(memory_space=pltpu.VMEM)


def smem():
    return pl.BlockSpec(memory_space=pltpu.SMEM)


def split2(x):
    hi = x.astype(BF16)
    return hi, (x - hi.astype(F32)).astype(BF16)


def split3(x):
    hi = x.astype(BF16)
    rest = x - hi.astype(F32)
    mid = rest.astype(BF16)
    return hi, mid, (rest - mid.astype(F32)).astype(BF16)


def prep_kernel(index_ref, taps_ref, col_ref, row_ref, order_ref, padded_ref):
    beams, taps = taps_ref.shape
    channels = index_ref.shape[0]
    padded_ref[...] = jnp.zeros_like(padded_ref)
    padded_ref[:, 0:taps] = taps_ref[...]
    table = padded_ref[...]
    table = table / jnp.sum(table, axis=1, keepdims=True)
    padded_ref[...] = table
    for beam in range(beams):
        line = jnp.broadcast_to(table[beam : beam + 1, :], (128, 256))
        band = pltpu.roll(line, 49, 1, stride=1, stride_axis=0)
        hi, mid = split2(band)
        col_ref[beam, 0:128, :] = hi
        col_ref[beam, 128:256, :] = mid
    lane = lax.broadcasted_iota(jnp.int32, (32, 256), 1)
    line_no = lax.broadcasted_iota(jnp.int32, (32, 256), 0)
    for channel in range(channels):
        line = jnp.broadcast_to(padded_ref[pl.ds(index_ref[channel], 1), :], (32, 256))
        band = pltpu.roll(line, 1, 1, stride=1, stride_axis=0)
        moved = pltpu.roll(band, 8, 1)
        band = jnp.where(lane < 32, band, jnp.where(lane < 40, 0.0, moved))
        band = jnp.where((lane < 64) & (line_no < 24), band, 0.0)
        group, place = channel // 4, channel % 4
        if place:
            band = pltpu.roll(band, 64 * place, 1)
        for part, value in enumerate(split3(band)):
            row_ref[group, part * 128 + place * 32 : part * 128 + place * 32 + 32, :] = value
    rows = order_ref.shape[0]
    out_row = lax.broadcasted_iota(jnp.int32, order_ref.shape, 0)
    in_row = lax.broadcasted_iota(jnp.int32, order_ref.shape, 1)
    count = rows // 24
    wanted = (out_row % count) * 32 + out_row // count
    order_ref[...] = jnp.where(in_row == wanted, 1.0, 0.0).astype(BF16)


def prepare(beam_index, beam_taps, chunk):
    channels = beam_index.shape[0]
    beams = beam_taps.shape[0]
    return pl.pallas_call(
        prep_kernel,
        out_shape=(
            jax.ShapeDtypeStruct((beams, 256, 256), BF16),
            jax.ShapeDtypeStruct((channels // 4, 384, 256), BF16),
            jax.ShapeDtypeStruct((chunk * 24, chunk * 32), BF16),
        ),
        in_specs=[smem(), vmem()],
        out_specs=(vmem(), vmem(), vmem()),
        scratch_shapes=[pltpu.VMEM((beams, 256), F32)],
        cost_estimate=pl.CostEstimate(flops=10**6, bytes_accessed=2 * 10**6, transcendentals=0),
        name="prep",
    )(beam_index, beam_taps)


def smooth_kernel(
    index_ref, before, top, bottom, after, col_ref, row_ref, order_ref, out_ref, hi_ref, mid_ref, sm_ref
):
    channels = before.shape[0]
    columns = before.shape[2]
    blocks = columns // 256
    tiles = columns // 128
    lane = lax.broadcasted_iota(jnp.int32, (128, 128), 1)
    for group in range(channels // 4):
        weights = row_ref[group]

        def row_step(n, tail):
            cols = pl.ds(pl.multiple_of(n * 256, 256), 256)
            data = jnp.concatenate(
                [
                    ref[group * 4 + place, :, cols]
                    for place in range(4)
                    for ref in (before, top, bottom, after)
                ],
                axis=0,
            )
            full = jnp.dot(weights, data, preferred_element_type=F32)
            value = full[0:128] + full[128:256] + full[256:384]
            moved = pltpu.roll(value, 64, 1)
            first = jnp.where(lane < 64, tail, moved[:, 0:128])
            for half, piece in ((0, first), (1, moved[:, 128:256])):
                hi, mid = split2(piece)
                for place in range(4):
                    rows = slice(place * 32, place * 32 + 32)
                    hi_ref[group * 4 + place, 2 * n + half] = hi[rows]
                    mid_ref[group * 4 + place, 2 * n + half] = mid[rows]
            return moved[:, 0:128]

        tail = lax.fori_loop(0, blocks, row_step, jnp.zeros((128, 128), F32))
        hi, mid = split2(jnp.where(lane < 64, tail, 0.0))
        for place in range(4):
            rows = slice(place * 32, place * 32 + 32)
            hi_ref[group * 4 + place, tiles] = hi[rows]
            mid_ref[group * 4 + place, tiles] = mid[rows]

    run = 16

    def col_step(channel, carry):
        band = col_ref[index_ref[channel]]
        rows = pl.ds(pl.multiple_of(channel * 32, 32), 32)
        for start in range(0, tiles, run):
            total = None
            for ref in (hi_ref, mid_ref):
                data = jnp.concatenate(
                    [
                        ref[channel, start : start + run].reshape(run * 32, 128),
                        ref[channel, start + 1 : start + run + 1].reshape(run * 32, 128),
                    ],
                    axis=1,
                )
                term = lax.dot_general(data, band, NT, preferred_element_type=F32)
                total = term if total is None else total + term
            value = (total[:, 0:128] + total[:, 128:256]).astype(BF16)
            sm_ref[start : start + run, rows, :] = value.reshape(run, 32, 128)
        return carry

    lax.fori_loop(0, channels, col_step, 0)

    lane3 = lax.broadcasted_iota(jnp.int32, (12, channels, 128), 2)

    def place_step(n, carry):
        data = jnp.concatenate([sm_ref[2 * n], sm_ref[2 * n + 1]], axis=1)
        moved = jnp.dot(order_ref[...], data, preferred_element_type=F32)
        for t in range(2):
            four = moved[:, t * 128 : t * 128 + 128].reshape(12, 2, channels, 128)
            even, odd = four[:, 0], four[:, 1]
            low = jnp.where(lane3 < 64, even, pltpu.roll(odd, 64, 2)).astype(BF16)
            high = jnp.where(lane3 < 64, pltpu.roll(even, 64, 2), odd).astype(BF16)
            for q in range(12):
                out_ref[4 * n + 2 * t, :, q * 128 : q * 128 + 128] = low[q]
                out_ref[4 * n + 2 * t + 1, :, q * 128 : q * 128 + 128] = high[q]
        return carry

    lax.fori_loop(0, blocks, place_step, 0)


def smooth(beam_index, before, top, bottom, after, col, row, order):
    channels, _, columns = before.shape
    tiles = columns // 128
    return pl.pallas_call(
        smooth_kernel,
        out_shape=jax.ShapeDtypeStruct((columns // 64, channels, 1536), BF16),
        in_specs=[smem()] + [vmem()] * 7,
        out_specs=vmem(),
        scratch_shapes=[
            pltpu.VMEM((channels, tiles + 1, 32, 128), BF16),
            pltpu.VMEM((channels, tiles + 1, 32, 128), BF16),
            pltpu.VMEM((tiles, channels * 32, 128), BF16),
        ],
        compiler_params=pltpu.CompilerParams(vmem_limit_bytes=VMEM_LIMIT),
        cost_estimate=pl.CostEstimate(
            flops=8 * 10**9, bytes_accessed=15 * 10**6, transcendentals=0
        ),
        name="smooth",
    )(beam_index, before, top, bottom, after, col, row, order)


def cov_kernel(core_ref, data_ref, keep_ref, send_ref):
    core = core_ref[0]

    def fill(out_ref, first):
        def step(i, carry):
            block = first + i
            left = data_ref[pl.ds(pl.multiple_of(block * 128, 128), 128), :]
            for d in range(5):
                other = lax.rem(block + d, 8)
                right = data_ref[pl.ds(pl.multiple_of(other * 128, 128), 128), :]
                out_ref[i, d * 128 : d * 128 + 128, :] = lax.dot_general(
                    left, right, NT, preferred_element_type=F32
                )
            return carry

        lax.fori_loop(0, 4, step, 0)

    fill(keep_ref, core * 4)
    fill(send_ref, (1 - core) * 4)


def local_covariance(core, data):
    shape = jax.ShapeDtypeStruct((4, 640, 128), F32)
    return pl.pallas_call(
        cov_kernel,
        out_shape=(shape, shape),
        in_specs=[smem(), vmem()],
        out_specs=(vmem(), vmem()),
        compiler_params=pltpu.CompilerParams(vmem_limit_bytes=VMEM_LIMIT),
        cost_estimate=pl.CostEstimate(
            flops=2 * 10**9, bytes_accessed=6 * 10**6, transcendentals=0
        ),
        name="cov",
    )(core, data)


def everywhere(x, axes, size):
    copies = jnp.broadcast_to(x[None], (size,) + x.shape)
    return lax.all_to_all(copies, axes, 0, 0, tiled=True)


def reduce_all(keep, send):
    swap = [(0, 1), (1, 0)]
    half = keep + lax.ppermute(send, "core", swap)
    got = lax.all_to_all(half.reshape(4, 640, 128), "sky", 0, 0, tiled=True)
    quarter = jnp.sum(got, axis=0)
    got = lax.all_to_all(quarter.reshape(32, 20, 128), ("y", "z"), 0, 0, tiled=True)
    mine = jnp.sum(got, axis=0)
    quarter = everywhere(mine, ("y", "z"), 32).reshape(640, 128)
    half = everywhere(quarter, "sky", 4).reshape(4, 640, 128)
    other = lax.ppermute(half, "core", swap)
    return half, other


def inverse_factor(gram):
    size = gram.shape[0]
    row = lax.broadcasted_iota(jnp.int32, (size, 128), 0)
    lane = lax.broadcasted_iota(jnp.int32, (size, 128), 1)
    unit = jnp.where(lane == row + size, 1.0, 0.0).astype(F32)
    work = jnp.concatenate([gram, jnp.zeros((size, 128 - size), F32)], axis=1) + unit
    for j in range(size):
        column = work[:, j : j + 1]
        factor = jnp.where(row[:, 0:1] > j, column, 0.0) * (1.0 / work[j : j + 1, j : j + 1])
        work = work - factor * work[j : j + 1, :]
    pivot = jnp.sum(jnp.where(lane == row, work, 0.0), axis=1, keepdims=True)
    scale = lax.rsqrt(pivot)
    scale = scale * (1.5 - 0.5 * pivot * scale * scale)
    return (work * scale)[:, size : 2 * size]


def clean_kernel(core_ref, near_ref, far_ref, seed_ref, data_ref, out_ref, cov_ref, basis_ref, coef_ref):
    core = core_ref[0]
    modes = seed_ref.shape[0]
    count = seed_ref.shape[1]
    pixels = data_ref.shape[1]
    scale = 1.0 / (256 * pixels)
    for i in range(8):
        for d in range(5):
            rows = slice(d * 128, d * 128 + 128)
            near, far = near_ref[i % 4, rows, :], far_ref[i % 4, rows, :]
            block = jnp.where(core == i // 4, near, far) * scale
            j = (i + d) % 8
            hi, mid = split2(block)
            cov_ref[i * 128 : i * 128 + 128, j * 128 : j * 128 + 128] = hi
            cov_ref[i * 128 : i * 128 + 128, count + j * 128 : count + j * 128 + 128] = mid
            if d in (1, 2, 3):
                hi, mid = split2(block.T)
                cov_ref[j * 128 : j * 128 + 128, i * 128 : i * 128 + 128] = hi
                cov_ref[j * 128 : j * 128 + 128, count + i * 128 : count + i * 128 + 128] = mid

    def fold(x):
        return x[0:modes] + x[modes : 2 * modes] + x[2 * modes : 3 * modes]

    def stack(x):
        return jnp.concatenate(split3(x), axis=0)

    def times_cov(parts):
        wide = fold(jnp.dot(parts, cov_ref[...], preferred_element_type=F32))
        return wide[:, 0:count] + wide[:, count : 2 * count]

    def gram_of(parts):
        tall = fold(lax.dot_general(parts, parts, NT, preferred_element_type=F32))
        return tall[:, 0:modes] + tall[:, modes : 2 * modes] + tall[:, 2 * modes : 3 * modes]

    def exact_dot(a, b):
        return lax.dot(a, b, precision=lax.Precision.HIGHEST, preferred_element_type=F32)

    images = times_cov(stack(seed_ref[...].astype(F32)))

    def sweep(step, images):
        parts = stack(images)
        inverse = inverse_factor(gram_of(parts))
        return exact_dot(inverse, times_cov(parts))

    images = lax.fori_loop(0, ITERS - 1, sweep, images)
    basis = exact_dot(inverse_factor(gram_of(stack(images))), images)
    hi, mid, low = split3(basis)
    basis_ref[...] = jnp.concatenate([hi, hi, mid, mid, hi, low], axis=0)
    data = data_ref[...]
    coef = fold(
        jnp.dot(jnp.concatenate([hi, mid, low], axis=0), data, preferred_element_type=F32)
    )
    hi, mid, low = split3(coef)
    coef_ref[...] = jnp.concatenate([hi, mid, hi, mid, low, hi], axis=0)
    for m in range(count // 128):
        rows = slice(m * 128, m * 128 + 128)
        part = lax.dot_general(
            basis_ref[:, rows], coef_ref[...], TN, preferred_element_type=F32
        )
        out_ref[rows, :] = (data_ref[rows, :].astype(F32) - part).astype(BF16)


def clean(core, near, far, seed, data):
    modes, count = seed.shape
    pixels = data.shape[1]
    return pl.pallas_call(
        clean_kernel,
        out_shape=jax.ShapeDtypeStruct((count, pixels), BF16),
        in_specs=[smem()] + [vmem()] * 4,
        out_specs=vmem(),
        scratch_shapes=[
            pltpu.VMEM((count, 2 * count), BF16),
            pltpu.VMEM((6 * modes, count), BF16),
            pltpu.VMEM((6 * modes, pixels), BF16),
        ],
        compiler_params=pltpu.CompilerParams(vmem_limit_bytes=VMEM_LIMIT),
        cost_estimate=pl.CostEstimate(
            flops=3 * 10**9, bytes_accessed=12 * 10**6, transcendentals=0
        ),
        name="clean",
    )(core, near, far, seed, data)


def body(sky_maps, beam_index, beam_taps, start_seed):
    channels, strip_rows, columns = sky_maps.shape
    core = lax.axis_index("core").astype(jnp.int32).reshape(1)
    top = sky_maps[:, 0:16, :]
    bottom = sky_maps[:, strip_rows - 16 : strip_rows, :]
    before = lax.ppermute(bottom, "sky", [(i, i + 1) for i in range(3)])
    after = lax.ppermute(top, "sky", [(i + 1, i) for i in range(3)])
    col, row, order = prepare(beam_index, beam_taps, channels)
    pieces = smooth(beam_index, before, top, bottom, after, col, row, order)
    data = lax.all_to_all(pieces, ("y", "z", "core"), 0, 0, tiled=True)
    data = data.reshape(64 * channels, 1536)
    keep, send = local_covariance(core, data)
    near, far = reduce_all(keep, send)
    cleaned = clean(core, near, far, start_seed.T, data)
    return cleaned[:, None, :]


def solution(mesh):
    fine = Mesh(mesh.devices.reshape(4, 8, 2, 4), ("y", "z", "core", "sky"))
    freq = ("y", "z", "core")
    return jax.shard_map(
        body,
        mesh=fine,
        in_specs=(P(freq, "sky", None), P(freq), P(), P()),
        out_specs=P(None, freq + ("sky",), None),
        check_vma=False,
    )
```

```python
import jax
import jax.numpy as jnp
from jax import lax
from jax.experimental import pallas as pl
from jax.experimental.pallas import tpu as pltpu
from jax.sharding import Mesh, PartitionSpec as P

ITERS = 8
F32 = jnp.float32
BF16 = jnp.bfloat16
NT = (((1,), (1,)), ((), ()))
TN = (((0,), (0,)), ((), ()))
ROW_UNROLL, COL_UNROLL, PLACE_UNROLL, COL_RUN = 16, 4, 16, 16
CHUNK = 8
VMEM_LIMIT = 60 * 1024 * 1024


def vmem():
    return pl.BlockSpec(memory_space=pltpu.VMEM)


def smem():
    return pl.BlockSpec(memory_space=pltpu.SMEM)


def split2(x):
    hi = x.astype(BF16)
    return hi, (x - hi.astype(F32)).astype(BF16)


def split3(x):
    hi = x.astype(BF16)
    rest = x - hi.astype(F32)
    mid = rest.astype(BF16)
    return hi, mid, (rest - mid.astype(F32)).astype(BF16)


def prep_kernel(index_ref, taps_ref, col_ref, row_ref, order_ref, padded_ref):
    beams, taps = taps_ref.shape
    channels = index_ref.shape[0]
    padded_ref[...] = jnp.zeros_like(padded_ref)
    padded_ref[:, 0:taps] = taps_ref[...]
    table = padded_ref[...]
    table = table / jnp.sum(table, axis=1, keepdims=True)
    padded_ref[...] = table
    for beam in range(beams):
        line = jnp.broadcast_to(table[beam : beam + 1, :], (128, 256))
        band = pltpu.roll(line, 49, 1, stride=1, stride_axis=0)
        hi, mid = split2(band)
        col_ref[beam, 0:128, :] = hi
        col_ref[beam, 128:256, :] = mid
    lane = lax.broadcasted_iota(jnp.int32, (32, 256), 1)
    line_no = lax.broadcasted_iota(jnp.int32, (32, 256), 0)
    for channel in range(channels):
        line = jnp.broadcast_to(padded_ref[pl.ds(index_ref[channel], 1), :], (32, 256))
        band = pltpu.roll(line, 1, 1, stride=1, stride_axis=0)
        moved = pltpu.roll(band, 8, 1)
        band = jnp.where(lane < 32, band, jnp.where(lane < 40, 0.0, moved))
        band = jnp.where((lane < 64) & (line_no < 24), band, 0.0)
        group, place = channel // 4, channel % 4
        if place:
            band = pltpu.roll(band, 64 * place, 1)
        for part, value in enumerate(split3(band)):
            row_ref[group, part * 128 + place * 32 : part * 128 + place * 32 + 32, :] = value
    rows = order_ref.shape[0]
    out_row = lax.broadcasted_iota(jnp.int32, order_ref.shape, 0)
    in_row = lax.broadcasted_iota(jnp.int32, order_ref.shape, 1)
    count = rows // 24
    wanted = (out_row % count) * 32 + out_row // count
    order_ref[...] = jnp.where(in_row == wanted, 1.0, 0.0).astype(BF16)


def prepare(beam_index, beam_taps, chunk):
    channels = beam_index.shape[0]
    beams = beam_taps.shape[0]
    return pl.pallas_call(
        prep_kernel,
        out_shape=(
            jax.ShapeDtypeStruct((beams, 256, 256), BF16),
            jax.ShapeDtypeStruct((channels // 4, 384, 256), BF16),
            jax.ShapeDtypeStruct((chunk * 24, chunk * 32), BF16),
        ),
        in_specs=[smem(), vmem()],
        out_specs=(vmem(), vmem(), vmem()),
        scratch_shapes=[pltpu.VMEM((beams, 256), F32)],
        cost_estimate=pl.CostEstimate(flops=10**6, bytes_accessed=2 * 10**6, transcendentals=0),
        name="prep",
    )(beam_index, beam_taps)


def smooth_kernel(
    index_ref, before, top, bottom, after, col_ref, row_ref, order_ref, out_ref, hi_ref, mid_ref, sm_ref
):
    group = pl.program_id(0)
    columns = before.shape[2]
    blocks = columns // 256
    tiles = columns // 128
    lane = lax.broadcasted_iota(jnp.int32, (128, 128), 1)

    def keep(tile, piece):
        hi, mid = split2(piece)
        for place in range(4):
            rows = slice(place * 32, place * 32 + 32)
            hi_ref[place, tile] = hi[rows]
            mid_ref[place, tile] = mid[rows]

    def row_step(n, tail):
        cols = pl.ds(pl.multiple_of(n * 256, 256), 256)
        data = jnp.concatenate(
            [ref[place, :, cols] for place in range(4) for ref in (before, top, bottom, after)],
            axis=0,
        )
        full = jnp.dot(row_ref[0], data, preferred_element_type=F32)
        value = full[0:128] + full[128:256] + full[256:384]
        moved = pltpu.roll(value, 64, 1)
        keep(2 * n, jnp.where(lane < 64, tail, moved[:, 0:128]))
        keep(2 * n + 1, moved[:, 128:256])
        return moved[:, 0:128]

    tail = lax.fori_loop(0, blocks, row_step, jnp.zeros((128, 128), F32), unroll=ROW_UNROLL)
    keep(tiles, jnp.where(lane < 64, tail, 0.0))

    def col_step(place, carry):
        channel = group * 4 + place
        band = col_ref[index_ref[channel]]
        rows = pl.ds(pl.multiple_of(channel * 32, 32), 32)
        for start in range(0, tiles, COL_RUN):
            total = None
            for ref in (hi_ref, mid_ref):
                data = jnp.concatenate(
                    [
                        ref[place, start : start + COL_RUN].reshape(COL_RUN * 32, 128),
                        ref[place, start + 1 : start + COL_RUN + 1].reshape(COL_RUN * 32, 128),
                    ],
                    axis=1,
                )
                term = lax.dot_general(data, band, NT, preferred_element_type=F32)
                total = term if total is None else total + term
            value = (total[:, 0:128] + total[:, 128:256]).astype(BF16)
            sm_ref[start : start + COL_RUN, rows, :] = value.reshape(COL_RUN, 32, 128)
        return carry

    lax.fori_loop(0, 4, col_step, 0, unroll=COL_UNROLL)

    @pl.when(group == pl.num_programs(0) - 1)
    def _():
        channels = out_ref.shape[1]
        lane3 = lax.broadcasted_iota(jnp.int32, (12, channels, 128), 2)

        def place_step(n, carry):
            data = jnp.concatenate([sm_ref[2 * n], sm_ref[2 * n + 1]], axis=1)
            moved = jnp.dot(order_ref[...], data, preferred_element_type=F32)
            for t in range(2):
                four = moved[:, t * 128 : t * 128 + 128].reshape(12, 2, channels, 128)
                even, odd = four[:, 0], four[:, 1]
                low = jnp.where(lane3 < 64, even, pltpu.roll(odd, 64, 2)).astype(BF16)
                high = jnp.where(lane3 < 64, pltpu.roll(even, 64, 2), odd).astype(BF16)
                for q in range(12):
                    out_ref[4 * n + 2 * t, :, q * 128 : q * 128 + 128] = low[q]
                    out_ref[4 * n + 2 * t + 1, :, q * 128 : q * 128 + 128] = high[q]
            return carry

        lax.fori_loop(0, blocks, place_step, 0, unroll=PLACE_UNROLL)


def smooth(beam_index, before, top, bottom, after, col, row, order):
    channels, _, columns = before.shape
    tiles = columns // 128
    strip = pl.BlockSpec((4, 16, columns), lambda g: (g, 0, 0))
    return pl.pallas_call(
        smooth_kernel,
        grid=(channels // 4,),
        out_shape=jax.ShapeDtypeStruct((columns // 64, channels, 1536), BF16),
        in_specs=[smem()]
        + [strip] * 4
        + [
            pl.BlockSpec(col.shape, lambda g: (0, 0, 0)),
            pl.BlockSpec((1,) + row.shape[1:], lambda g: (g, 0, 0)),
            pl.BlockSpec(order.shape, lambda g: (0, 0)),
        ],
        out_specs=pl.BlockSpec((columns // 64, channels, 1536), lambda g: (0, 0, 0)),
        scratch_shapes=[
            pltpu.VMEM((4, tiles + 1, 32, 128), BF16),
            pltpu.VMEM((4, tiles + 1, 32, 128), BF16),
            pltpu.VMEM((tiles, channels * 32, 128), BF16),
        ],
        compiler_params=pltpu.CompilerParams(vmem_limit_bytes=VMEM_LIMIT),
        cost_estimate=pl.CostEstimate(
            flops=5 * 10**8 * channels, bytes_accessed=10**6 * channels, transcendentals=0
        ),
        name="smooth",
    )(beam_index, before, top, bottom, after, col, row, order)


def load_parts(parts, data_ref, sems):
    copies, first = [], 0
    for k, part in enumerate(parts):
        rows = part.shape[0]
        copies.append(
            pltpu.make_async_copy(part, data_ref.at[first : first + rows], sems.at[k])
        )
        first += rows
    for copy in copies:
        copy.start()
    return copies


def cov_kernel(core_ref, part0, part1, keep_ref, send_ref, data_ref, sems):
    for copy in load_parts((part0, part1), data_ref, sems):
        copy.wait()
    core = core_ref[0]

    def fill(out_ref, first):
        def step(i, carry):
            block = first + i
            left = data_ref[pl.ds(pl.multiple_of(block * 128, 128), 128), :]
            for d in range(5):
                other = lax.rem(block + d, 8)
                right = data_ref[pl.ds(pl.multiple_of(other * 128, 128), 128), :]
                out_ref[i, d * 128 : d * 128 + 128, :] = lax.dot_general(
                    left, right, NT, preferred_element_type=F32
                )
            return carry

        lax.fori_loop(0, 4, step, 0)

    fill(keep_ref, core * 4)
    fill(send_ref, (1 - core) * 4)


def anywhere():
    return pl.BlockSpec(memory_space=pl.ANY)


def local_covariance(core, parts):
    shape = jax.ShapeDtypeStruct((4, 640, 128), F32)
    rows = sum(part.shape[0] for part in parts)
    return pl.pallas_call(
        cov_kernel,
        out_shape=(shape, shape),
        in_specs=[smem(), anywhere(), anywhere()],
        out_specs=(vmem(), vmem()),
        scratch_shapes=[
            pltpu.VMEM((rows, parts[0].shape[1]), BF16),
            pltpu.SemaphoreType.DMA((2,)),
        ],
        compiler_params=pltpu.CompilerParams(vmem_limit_bytes=VMEM_LIMIT),
        cost_estimate=pl.CostEstimate(
            flops=2 * 10**9, bytes_accessed=6 * 10**6, transcendentals=0
        ),
        name="cov",
    )(core, *parts)


def everywhere(x, axes, size):
    copies = jnp.broadcast_to(x[None], (size,) + x.shape)
    return lax.all_to_all(copies, axes, 0, 0, tiled=True)


def reduce_all(keep, send):
    swap = [(0, 1), (1, 0)]
    half = keep + lax.ppermute(send, "core", swap)
    got = lax.all_to_all(half.reshape(4, 640, 128), "sky", 0, 0, tiled=True)
    quarter = jnp.sum(got, axis=0)
    got = lax.all_to_all(quarter.reshape(32, 20, 128), ("y", "z"), 0, 0, tiled=True)
    mine = jnp.sum(got, axis=0)
    quarter = everywhere(mine, ("y", "z"), 32).reshape(640, 128)
    half = everywhere(quarter, "sky", 4).reshape(4, 640, 128)
    other = lax.ppermute(half, "core", swap)
    return half, other


def inverse_factor(gram):
    size = gram.shape[0]
    row = lax.broadcasted_iota(jnp.int32, (size, 128), 0)
    lane = lax.broadcasted_iota(jnp.int32, (size, 128), 1)
    unit = jnp.where(lane == row + size, 1.0, 0.0).astype(F32)
    work = jnp.concatenate([gram, jnp.zeros((size, 128 - size), F32)], axis=1) + unit
    for j in range(size):
        column = work[:, j : j + 1]
        factor = jnp.where(row[:, 0:1] > j, column, 0.0) * (1.0 / work[j : j + 1, j : j + 1])
        work = work - factor * work[j : j + 1, :]
    pivot = jnp.sum(jnp.where(lane == row, work, 0.0), axis=1, keepdims=True)
    scale = lax.rsqrt(pivot)
    scale = scale * (1.5 - 0.5 * pivot * scale * scale)
    return (work * scale)[:, size : 2 * size]


def clean_kernel(
    core_ref, near_ref, far_ref, seed_ref, part0, part1, out_ref, data_ref, cov_ref, basis_ref, coef_ref, sems
):
    core = core_ref[0]
    copies = load_parts((part0, part1), data_ref, sems)
    modes = seed_ref.shape[0]
    count = seed_ref.shape[1]
    pixels = data_ref.shape[1]
    scale = 1.0 / (256 * pixels)
    for i in range(8):
        for d in range(5):
            rows = slice(d * 128, d * 128 + 128)
            near, far = near_ref[i % 4, rows, :], far_ref[i % 4, rows, :]
            block = jnp.where(core == i // 4, near, far) * scale
            j = (i + d) % 8
            hi, mid = split2(block)
            cov_ref[i * 128 : i * 128 + 128, j * 128 : j * 128 + 128] = hi
            cov_ref[i * 128 : i * 128 + 128, count + j * 128 : count + j * 128 + 128] = mid
            if d in (1, 2, 3):
                hi, mid = split2(block.T)
                cov_ref[j * 128 : j * 128 + 128, i * 128 : i * 128 + 128] = hi
                cov_ref[j * 128 : j * 128 + 128, count + i * 128 : count + i * 128 + 128] = mid

    def fold(x):
        return x[0:modes] + x[modes : 2 * modes] + x[2 * modes : 3 * modes]

    def stack(x):
        return jnp.concatenate(split3(x), axis=0)

    def times_cov(parts):
        wide = fold(jnp.dot(parts, cov_ref[...], preferred_element_type=F32))
        return wide[:, 0:count] + wide[:, count : 2 * count]

    def gram_of(parts):
        tall = fold(lax.dot_general(parts, parts, NT, preferred_element_type=F32))
        return tall[:, 0:modes] + tall[:, modes : 2 * modes] + tall[:, 2 * modes : 3 * modes]

    def exact_dot(a, b):
        return lax.dot(a, b, precision=lax.Precision.HIGHEST, preferred_element_type=F32)

    images = times_cov(stack(seed_ref[...].astype(F32)))

    def sweep(step, images):
        parts = stack(images)
        inverse = inverse_factor(gram_of(parts))
        return exact_dot(inverse, times_cov(parts))

    images = lax.fori_loop(0, ITERS - 1, sweep, images)
    basis = exact_dot(inverse_factor(gram_of(stack(images))), images)
    hi, mid, low = split3(basis)
    basis_ref[...] = jnp.concatenate([hi, hi, mid, mid, hi, low], axis=0)
    for copy in copies:
        copy.wait()
    data = data_ref[...]
    coef = fold(
        jnp.dot(jnp.concatenate([hi, mid, low], axis=0), data, preferred_element_type=F32)
    )
    hi, mid, low = split3(coef)
    coef_ref[...] = jnp.concatenate([hi, mid, hi, mid, low, hi], axis=0)
    for m in range(count // 128):
        rows = slice(m * 128, m * 128 + 128)
        part = lax.dot_general(
            basis_ref[:, rows], coef_ref[...], TN, preferred_element_type=F32
        )
        value = (data_ref[rows, :].astype(F32) - part).astype(BF16)
        chunk, first = m // 4, (m % 4) * 16
        out_ref[first : first + 16, chunk * 8 : chunk * 8 + 8, :] = value.reshape(16, 8, pixels)


def clean(core, near, far, seed, parts):
    modes, count = seed.shape
    pixels = parts[0].shape[1]
    return pl.pallas_call(
        clean_kernel,
        out_shape=jax.ShapeDtypeStruct((count // 16, 16, pixels), BF16),
        in_specs=[smem()] + [vmem()] * 3 + [anywhere(), anywhere()],
        out_specs=vmem(),
        scratch_shapes=[
            pltpu.VMEM((count, pixels), BF16),
            pltpu.VMEM((count, 2 * count), BF16),
            pltpu.VMEM((6 * modes, count), BF16),
            pltpu.VMEM((6 * modes, pixels), BF16),
            pltpu.SemaphoreType.DMA((2,)),
        ],
        compiler_params=pltpu.CompilerParams(vmem_limit_bytes=VMEM_LIMIT),
        cost_estimate=pl.CostEstimate(
            flops=3 * 10**9, bytes_accessed=12 * 10**6, transcendentals=0
        ),
        name="clean",
    )(core, near, far, seed, *parts)


def body(sky_maps, beam_index, beam_taps, start_seed):
    channels, strip_rows, columns = sky_maps.shape
    modes = start_seed.shape[1]
    core = lax.axis_index("core").astype(jnp.int32).reshape(1)
    col, row, order = prepare(beam_index, beam_taps, CHUNK)
    halos = []
    for first in range(0, channels, CHUNK):
        strip = sky_maps[first : first + CHUNK]
        top = strip[:, 0:16, :]
        bottom = strip[:, strip_rows - 16 : strip_rows, :]
        before = lax.ppermute(bottom, "sky", [(i, i + 1) for i in range(3)])
        after = lax.ppermute(top, "sky", [(i + 1, i) for i in range(3)])
        halos.append((before, top, bottom, after))
    parts = []
    for k, halo in enumerate(halos):
        mine = slice(k * CHUNK, (k + 1) * CHUNK)
        rows = row[k * CHUNK // 4 : (k + 1) * CHUNK // 4]
        pieces = smooth(beam_index[mine], *halo, col, rows, order)
        data = lax.all_to_all(pieces, ("y", "z", "core"), 0, 0, tiled=True)
        parts.append(data.reshape(64 * CHUNK, 1536))
    seed = start_seed.T.reshape(modes, 64, channels // CHUNK, CHUNK)
    seed = seed.transpose(0, 2, 1, 3).reshape(modes, 64 * channels)
    keep, send = local_covariance(core, parts)
    near, far = reduce_all(keep, send)
    cleaned = clean(core, near, far, seed, parts)
    return cleaned.reshape(64 * channels, 1, 1536)


def solution(mesh):
    fine = Mesh(mesh.devices.reshape(4, 8, 2, 4), ("y", "z", "core", "sky"))
    freq = ("y", "z", "core")
    return jax.shard_map(
        body,
        mesh=fine,
        in_specs=(P(freq, "sky", None), P(freq), P(), P()),
        out_specs=P(None, freq + ("sky",), None),
        check_vma=False,
    )
```

```python
import jax
import jax.numpy as jnp
from jax import lax
from jax.experimental import pallas as pl
from jax.experimental.pallas import tpu as pltpu
from jax.sharding import Mesh, PartitionSpec as P


ITERS = 8
F32 = jnp.float32
BF16 = jnp.bfloat16
NT = (((1,), (1,)), ((), ()))
TN = (((0,), (0,)), ((), ()))
ROW_UNROLL, COL_UNROLL, PLACE_UNROLL, COL_RUN = 16, 4, 16, 16
CHUNK = 8
VMEM_LIMIT = 60 * 1024 * 1024


def vmem():
    return pl.BlockSpec(memory_space=pltpu.VMEM)


def smem():
    return pl.BlockSpec(memory_space=pltpu.SMEM)


def split2(x):
    hi = x.astype(BF16)
    return hi, (x - hi.astype(F32)).astype(BF16)


def split3(x):
    hi = x.astype(BF16)
    rest = x - hi.astype(F32)
    mid = rest.astype(BF16)
    return hi, mid, (rest - mid.astype(F32)).astype(BF16)


def prep_kernel(index_ref, taps_ref, col_ref, row_ref, order_ref, padded_ref):
    beams, taps = taps_ref.shape
    channels = index_ref.shape[0]
    padded_ref[...] = jnp.zeros_like(padded_ref)
    padded_ref[:, 0:taps] = taps_ref[...]
    table = padded_ref[...]
    table = table / jnp.sum(table, axis=1, keepdims=True)
    padded_ref[...] = table
    for beam in range(beams):
        line = jnp.broadcast_to(table[beam : beam + 1, :], (128, 256))
        band = pltpu.roll(line, 49, 1, stride=1, stride_axis=0)
        hi, mid = split2(band)
        col_ref[beam, 0:128, :] = hi
        col_ref[beam, 128:256, :] = mid
    lane = lax.broadcasted_iota(jnp.int32, (32, 256), 1)
    line_no = lax.broadcasted_iota(jnp.int32, (32, 256), 0)
    for channel in range(channels):
        line = jnp.broadcast_to(padded_ref[pl.ds(index_ref[channel], 1), :], (32, 256))
        band = pltpu.roll(line, 1, 1, stride=1, stride_axis=0)
        moved = pltpu.roll(band, 8, 1)
        band = jnp.where(lane < 32, band, jnp.where(lane < 40, 0.0, moved))
        band = jnp.where((lane < 64) & (line_no < 24), band, 0.0)
        group, place = channel // 4, channel % 4
        if place:
            band = pltpu.roll(band, 64 * place, 1)
        for part, value in enumerate(split3(band)):
            row_ref[group, part * 128 + place * 32 : part * 128 + place * 32 + 32, :] = value
    rows = order_ref.shape[0]
    out_row = lax.broadcasted_iota(jnp.int32, order_ref.shape, 0)
    in_row = lax.broadcasted_iota(jnp.int32, order_ref.shape, 1)
    count = rows // 24
    wanted = (out_row % count) * 32 + out_row // count
    order_ref[...] = jnp.where(in_row == wanted, 1.0, 0.0).astype(BF16)


def prepare(beam_index, beam_taps, chunk):
    channels = beam_index.shape[0]
    beams = beam_taps.shape[0]
    return pl.pallas_call(
        prep_kernel,
        out_shape=(
            jax.ShapeDtypeStruct((beams, 256, 256), BF16),
            jax.ShapeDtypeStruct((channels // 4, 384, 256), BF16),
            jax.ShapeDtypeStruct((chunk * 24, chunk * 32), BF16),
        ),
        in_specs=[smem(), vmem()],
        out_specs=(vmem(), vmem(), vmem()),
        scratch_shapes=[pltpu.VMEM((beams, 256), F32)],
        cost_estimate=pl.CostEstimate(flops=10**6, bytes_accessed=2 * 10**6, transcendentals=0),
        name="prep",
    )(beam_index, beam_taps)


def smooth_kernel(
    index_ref, before, top, bottom, after, col_ref, row_ref, order_ref, out_ref, hi_ref, mid_ref, sm_ref
):
    group = pl.program_id(0)
    columns = before.shape[2]
    blocks = columns // 256
    tiles = columns // 128
    lane = lax.broadcasted_iota(jnp.int32, (128, 128), 1)

    def keep(tile, piece):
        hi, mid = split2(piece)
        for place in range(4):
            rows = slice(place * 32, place * 32 + 32)
            hi_ref[place, tile] = hi[rows]
            mid_ref[place, tile] = mid[rows]

    def row_step(n, tail):
        cols = pl.ds(pl.multiple_of(n * 256, 256), 256)
        data = jnp.concatenate(
            [ref[place, :, cols] for place in range(4) for ref in (before, top, bottom, after)],
            axis=0,
        )
        full = jnp.dot(row_ref[0], data, preferred_element_type=F32)
        value = full[0:128] + full[128:256] + full[256:384]
        moved = pltpu.roll(value, 64, 1)
        keep(2 * n, jnp.where(lane < 64, tail, moved[:, 0:128]))
        keep(2 * n + 1, moved[:, 128:256])
        return moved[:, 0:128]

    tail = lax.fori_loop(0, blocks, row_step, jnp.zeros((128, 128), F32), unroll=ROW_UNROLL)
    keep(tiles, jnp.where(lane < 64, tail, 0.0))

    def col_step(place, carry):
        channel = group * 4 + place
        band = col_ref[index_ref[channel]]
        rows = pl.ds(pl.multiple_of(channel * 32, 32), 32)
        for start in range(0, tiles, COL_RUN):
            total = None
            for ref in (hi_ref, mid_ref):
                data = jnp.concatenate(
                    [
                        ref[place, start : start + COL_RUN].reshape(COL_RUN * 32, 128),
                        ref[place, start + 1 : start + COL_RUN + 1].reshape(COL_RUN * 32, 128),
                    ],
                    axis=1,
                )
                term = lax.dot_general(data, band, NT, preferred_element_type=F32)
                total = term if total is None else total + term
            value = (total[:, 0:128] + total[:, 128:256]).astype(BF16)
            sm_ref[start : start + COL_RUN, rows, :] = value.reshape(COL_RUN, 32, 128)
        return carry

    lax.fori_loop(0, 4, col_step, 0, unroll=COL_UNROLL)

    @pl.when(group == pl.num_programs(0) - 1)
    def _():
        channels = out_ref.shape[1]
        lane3 = lax.broadcasted_iota(jnp.int32, (12, channels, 128), 2)

        def place_step(n, carry):
            data = jnp.concatenate([sm_ref[2 * n], sm_ref[2 * n + 1]], axis=1)
            moved = jnp.dot(order_ref[...], data, preferred_element_type=F32)
            for t in range(2):
                four = moved[:, t * 128 : t * 128 + 128].reshape(12, 2, channels, 128)
                even, odd = four[:, 0], four[:, 1]
                low = jnp.where(lane3 < 64, even, pltpu.roll(odd, 64, 2)).astype(BF16)
                high = jnp.where(lane3 < 64, pltpu.roll(even, 64, 2), odd).astype(BF16)
                for q in range(12):
                    out_ref[4 * n + 2 * t, :, q * 128 : q * 128 + 128] = low[q]
                    out_ref[4 * n + 2 * t + 1, :, q * 128 : q * 128 + 128] = high[q]
            return carry

        lax.fori_loop(0, blocks, place_step, 0, unroll=PLACE_UNROLL)


def smooth(beam_index, before, top, bottom, after, col, row, order):
    channels, _, columns = before.shape
    tiles = columns // 128
    strip = pl.BlockSpec((4, 16, columns), lambda g: (g, 0, 0))
    return pl.pallas_call(
        smooth_kernel,
        grid=(channels // 4,),
        out_shape=jax.ShapeDtypeStruct((columns // 64, channels, 1536), BF16),
        in_specs=[smem()]
        + [strip] * 4
        + [
            pl.BlockSpec(col.shape, lambda g: (0, 0, 0)),
            pl.BlockSpec((1,) + row.shape[1:], lambda g: (g, 0, 0)),
            pl.BlockSpec(order.shape, lambda g: (0, 0)),
        ],
        out_specs=pl.BlockSpec((columns // 64, channels, 1536), lambda g: (0, 0, 0)),
        scratch_shapes=[
            pltpu.VMEM((4, tiles + 1, 32, 128), BF16),
            pltpu.VMEM((4, tiles + 1, 32, 128), BF16),
            pltpu.VMEM((tiles, channels * 32, 128), BF16),
        ],
        compiler_params=pltpu.CompilerParams(vmem_limit_bytes=VMEM_LIMIT),
        cost_estimate=pl.CostEstimate(
            flops=5 * 10**8 * channels, bytes_accessed=10**6 * channels, transcendentals=0
        ),
        name="smooth",
    )(beam_index, before, top, bottom, after, col, row, order)


def load_parts(parts, data_ref, sems):
    copies, first = [], 0
    for k, part in enumerate(parts):
        rows = part.shape[0]
        copies.append(
            pltpu.make_async_copy(part, data_ref.at[first : first + rows], sems.at[k])
        )
        first += rows
    for copy in copies:
        copy.start()
    return copies


def cov_kernel(core_ref, part0, part1, keep_ref, send_ref, data_ref, sems):
    for copy in load_parts((part0, part1, part0), data_ref, sems):
        copy.wait()
    core = core_ref[0]

    def fill(out_ref, first):
        for unit in range(2):
            start = pl.multiple_of((first + 2 * unit) * 128, 256)
            wide = lax.dot_general(
                data_ref[pl.ds(start, 768), :],
                data_ref[pl.ds(start, 256), :],
                NT,
                preferred_element_type=F32,
            ).astype(out_ref.dtype)
            out_ref[2 * unit] = wide[0:640, 0:128]
            out_ref[2 * unit + 1] = wide[128:768, 128:256]

    fill(keep_ref, core * 4)
    fill(send_ref, (1 - core) * 4)


def anywhere():
    return pl.BlockSpec(memory_space=pl.ANY)


def local_covariance(core, parts):
    rows = sum(part.shape[0] for part in parts)
    return pl.pallas_call(
        cov_kernel,
        out_shape=(
            jax.ShapeDtypeStruct((4, 640, 128), F32),
            jax.ShapeDtypeStruct((4, 640, 128), BF16),
        ),
        in_specs=[smem(), anywhere(), anywhere()],
        out_specs=(vmem(), vmem()),
        scratch_shapes=[
            pltpu.VMEM((rows + parts[0].shape[0], parts[0].shape[1]), BF16),
            pltpu.SemaphoreType.DMA((3,)),
        ],
        compiler_params=pltpu.CompilerParams(vmem_limit_bytes=VMEM_LIMIT),
        cost_estimate=pl.CostEstimate(
            flops=2 * 10**9, bytes_accessed=6 * 10**6, transcendentals=0
        ),
        name="cov",
    )(core, *parts)


def everywhere(x, axes, size):
    copies = jnp.broadcast_to(x[None], (size,) + x.shape)
    return lax.all_to_all(copies, axes, 0, 0, tiled=True)


def reduce_all(keep, send):
    swap = [(0, 1), (1, 0)]
    half = (keep + lax.ppermute(send, "core", swap).astype(F32)).astype(BF16)
    got = lax.all_to_all(half.reshape(4, 640, 128), "sky", 0, 0, tiled=True)
    quarter = jnp.sum(got.astype(F32), axis=0).astype(BF16)
    got = lax.all_to_all(quarter.reshape(32, 20, 128), ("y", "z"), 0, 0, tiled=True)
    mine = jnp.sum(got.astype(F32), axis=0)
    quarter = everywhere(mine, ("y", "z"), 32).reshape(640, 128)
    half = everywhere(quarter, "sky", 4).reshape(4, 640, 128)
    other = lax.ppermute(half, "core", swap)
    return half, other


def inverse_factor(gram):
    size = gram.shape[0]
    row = lax.broadcasted_iota(jnp.int32, (size, 128), 0)
    lane = lax.broadcasted_iota(jnp.int32, (size, 128), 1)
    unit = jnp.where(lane == row + size, 1.0, 0.0).astype(F32)
    work = jnp.concatenate([gram, jnp.zeros((size, 128 - size), F32)], axis=1) + unit
    for j in range(size):
        column = work[:, j : j + 1]
        factor = jnp.where(row[:, 0:1] > j, column, 0.0) * (1.0 / work[j : j + 1, j : j + 1])
        work = work - factor * work[j : j + 1, :]
    pivot = jnp.sum(jnp.where(lane == row, work, 0.0), axis=1, keepdims=True)
    scale = lax.rsqrt(pivot)
    scale = scale * (1.5 - 0.5 * pivot * scale * scale)
    return (work * scale)[:, size : 2 * size]


def clean_kernel(
    core_ref, near_ref, far_ref, seed_ref, part0, part1, out_ref, data_ref, cov_ref, basis_ref, coef_ref, sems
):
    core = core_ref[0]
    copies = load_parts((part0, part1), data_ref, sems)
    modes = seed_ref.shape[0] // 3
    count = seed_ref.shape[1]
    pixels = data_ref.shape[1]
    scale = 1.0 / (256 * pixels)
    for i in range(8):
        for d in range(5):
            rows = slice(d * 128, d * 128 + 128)
            near, far = near_ref[i % 4, rows, :], far_ref[i % 4, rows, :]
            block = jnp.where(core == i // 4, near, far) * scale
            j = (i + d) % 8
            hi, mid = split2(block)
            cov_ref[j * 128 : j * 128 + 128, i * 128 : i * 128 + 128] = hi
            cov_ref[j * 128 : j * 128 + 128, count + i * 128 : count + i * 128 + 128] = mid
            if d in (1, 2, 3):
                hi, mid = split2(block.T)
                cov_ref[i * 128 : i * 128 + 128, j * 128 : j * 128 + 128] = hi
                cov_ref[i * 128 : i * 128 + 128, count + j * 128 : count + j * 128 + 128] = mid

    def fold(x):
        return x[0:modes] + x[modes : 2 * modes] + x[2 * modes : 3 * modes]

    def stack(x):
        return jnp.concatenate(split3(x), axis=0)

    def times_cov(parts):
        wide = fold(jnp.dot(parts, cov_ref[...], preferred_element_type=F32))
        return wide[:, 0:count] + wide[:, count : 2 * count]

    def gram_of(parts):
        tall = fold(lax.dot_general(parts, parts, NT, preferred_element_type=F32))
        return tall[:, 0:modes] + tall[:, modes : 2 * modes] + tall[:, 2 * modes : 3 * modes]

    def exact_dot(a, b):
        return lax.dot(a, b, precision=lax.Precision.HIGHEST, preferred_element_type=F32)

    images = times_cov(seed_ref[...])

    def sweep(step, images):
        parts = stack(images)
        inverse = inverse_factor(gram_of(parts))
        return exact_dot(inverse, times_cov(parts))

    images = lax.fori_loop(0, ITERS - 1, sweep, images)
    basis = exact_dot(inverse_factor(gram_of(stack(images))), images)
    hi, mid, low = split3(basis)
    basis_ref[...] = jnp.concatenate([hi, hi, mid, mid, hi, low], axis=0)
    for copy in copies:
        copy.wait()
    data = data_ref[...]
    coef = fold(
        jnp.dot(jnp.concatenate([hi, mid, low], axis=0), data, preferred_element_type=F32)
    )
    hi, mid, low = split3(coef)
    coef_ref[...] = jnp.concatenate([hi, mid, hi, mid, low, hi], axis=0)
    for m in range(count // 128):
        rows = slice(m * 128, m * 128 + 128)
        part = lax.dot_general(
            basis_ref[:, rows], coef_ref[...], TN, preferred_element_type=F32
        )
        value = (data_ref[rows, :].astype(F32) - part).astype(BF16)
        chunk, first = m // 4, (m % 4) * 16
        out_ref[first : first + 16, chunk * 8 : chunk * 8 + 8, :] = value.reshape(16, 8, pixels)


def seeds_kernel(seed_ref, out_ref):
    out_ref[...] = jnp.concatenate(split3(seed_ref[...].astype(F32)), axis=0)


def split_seed(seed):
    modes, count = seed.shape
    return pl.pallas_call(
        seeds_kernel,
        out_shape=jax.ShapeDtypeStruct((3 * modes, count), BF16),
        in_specs=[vmem()],
        out_specs=vmem(),
        name="seeds",
    )(seed)


def clean(core, near, far, seed, parts):
    modes, count = seed.shape
    modes = modes // 3
    pixels = parts[0].shape[1]
    return pl.pallas_call(
        clean_kernel,
        out_shape=jax.ShapeDtypeStruct((count // 16, 16, pixels), BF16),
        in_specs=[smem()] + [vmem()] * 3 + [anywhere(), anywhere()],
        out_specs=vmem(),
        scratch_shapes=[
            pltpu.VMEM((count, pixels), BF16),
            pltpu.VMEM((count, 2 * count), BF16),
            pltpu.VMEM((6 * modes, count), BF16),
            pltpu.VMEM((6 * modes, pixels), BF16),
            pltpu.SemaphoreType.DMA((2,)),
        ],
        compiler_params=pltpu.CompilerParams(vmem_limit_bytes=VMEM_LIMIT),
        cost_estimate=pl.CostEstimate(
            flops=3 * 10**9, bytes_accessed=12 * 10**6, transcendentals=0
        ),
        name="clean",
    )(core, near, far, seed, *parts)


def body(sky_maps, beam_index, beam_taps, start_seed):
    channels, strip_rows, _ = sky_maps.shape
    modes = start_seed.shape[1]
    core = lax.axis_index("core").astype(jnp.int32).reshape(1)
    col, row, order = prepare(beam_index, beam_taps, CHUNK)
    halos = []
    for first in range(0, channels, CHUNK):
        strip = sky_maps if first == 0 else lax.optimization_barrier(sky_maps)
        strip = strip[first : first + CHUNK]
        top = strip[:, 0:16, :]
        bottom = strip[:, strip_rows - 16 : strip_rows, :]
        k = first // CHUNK
        before = lax.ppermute(bottom, "sky", [(i, i + 1) for i in range(3)])
        after = lax.ppermute(top, "sky", [(i + 1, i) for i in range(3)])
        halos.append((before, top, bottom, after))
    parts = []
    for k, halo in enumerate(halos):
        mine = slice(k * CHUNK, (k + 1) * CHUNK)
        rows = row[k * CHUNK // 4 : (k + 1) * CHUNK // 4]
        pieces = smooth(beam_index[mine], *halo, col, rows, order)
        data = lax.all_to_all(pieces, ("y", "z", "core"), 0, 0, tiled=True)
        parts.append(data.reshape(64 * CHUNK, 1536))
    seed = start_seed.T.reshape(modes, 64, channels // CHUNK, CHUNK)
    seed = seed.transpose(0, 2, 1, 3).reshape(modes, 64 * channels)
    seed = split_seed(seed)
    keep, send = local_covariance(core, parts)
    near, far = reduce_all(keep, send)
    cleaned = clean(core, near, far, seed, parts)
    return cleaned.reshape(64 * channels, 1, 1536)


def solution(mesh):
    fine = Mesh(mesh.devices.reshape(4, 8, 2, 4), ("y", "z", "core", "sky"))
    freq = ("y", "z", "core")

    return jax.shard_map(
        body,
        mesh=fine,
        in_specs=(P(freq, "sky", None), P(freq), P(), P()),
        out_specs=P(None, freq + ("sky",), None),
        check_vma=False,
    )
```

```python
import jax
import jax.numpy as jnp
from jax import lax
from jax.experimental import pallas as pl
from jax.experimental.pallas import tpu as pltpu
from jax.sharding import Mesh, PartitionSpec as P


ITERS = 8
F32 = jnp.float32
BF16 = jnp.bfloat16
NT = (((1,), (1,)), ((), ()))
TN = (((0,), (0,)), ((), ()))
ROW_UNROLL, COL_UNROLL, PLACE_UNROLL, COL_RUN = 16, 4, 16, 16
CHUNK = 8
VMEM_LIMIT = 60 * 1024 * 1024


def vmem():
    return pl.BlockSpec(memory_space=pltpu.VMEM)


def smem():
    return pl.BlockSpec(memory_space=pltpu.SMEM)


def split2(x):
    hi = x.astype(BF16)
    return hi, (x - hi.astype(F32)).astype(BF16)


def split3(x):
    hi = x.astype(BF16)
    rest = x - hi.astype(F32)
    mid = rest.astype(BF16)
    return hi, mid, (rest - mid.astype(F32)).astype(BF16)


def prep_kernel(index_ref, taps_ref, col_ref, row_ref, order_ref, padded_ref):
    beams, taps = taps_ref.shape
    channels = index_ref.shape[0]
    padded_ref[...] = jnp.zeros_like(padded_ref)
    padded_ref[:, 0:taps] = taps_ref[...]
    table = padded_ref[...]
    table = table / jnp.sum(table, axis=1, keepdims=True)
    padded_ref[...] = table
    for beam in range(beams):
        line = jnp.broadcast_to(table[beam : beam + 1, :], (128, 256))
        band = pltpu.roll(line, 49, 1, stride=1, stride_axis=0)
        hi, mid = split2(band)
        col_ref[beam, 0:128, :] = hi
        col_ref[beam, 128:256, :] = mid
    lane = lax.broadcasted_iota(jnp.int32, (32, 256), 1)
    line_no = lax.broadcasted_iota(jnp.int32, (32, 256), 0)
    for channel in range(channels):
        line = jnp.broadcast_to(padded_ref[pl.ds(index_ref[channel], 1), :], (32, 256))
        band = pltpu.roll(line, 1, 1, stride=1, stride_axis=0)
        moved = pltpu.roll(band, 8, 1)
        band = jnp.where(lane < 32, band, jnp.where(lane < 40, 0.0, moved))
        band = jnp.where((lane < 64) & (line_no < 24), band, 0.0)
        group, place = channel // 4, channel % 4
        if place:
            band = pltpu.roll(band, 64 * place, 1)
        for part, value in enumerate(split3(band)):
            row_ref[group, part * 128 + place * 32 : part * 128 + place * 32 + 32, :] = value
    rows = order_ref.shape[0]
    out_row = lax.broadcasted_iota(jnp.int32, order_ref.shape, 0)
    in_row = lax.broadcasted_iota(jnp.int32, order_ref.shape, 1)
    count = rows // 24
    wanted = (out_row % count) * 32 + out_row // count
    order_ref[...] = jnp.where(in_row == wanted, 1.0, 0.0).astype(BF16)


def prepare(beam_index, beam_taps, chunk):
    channels = beam_index.shape[0]
    beams = beam_taps.shape[0]
    return pl.pallas_call(
        prep_kernel,
        out_shape=(
            jax.ShapeDtypeStruct((beams, 256, 256), BF16),
            jax.ShapeDtypeStruct((channels // 4, 384, 256), BF16),
            jax.ShapeDtypeStruct((chunk * 24, chunk * 32), BF16),
        ),
        in_specs=[smem(), vmem()],
        out_specs=(vmem(), vmem(), vmem()),
        scratch_shapes=[pltpu.VMEM((beams, 256), F32)],
        cost_estimate=pl.CostEstimate(flops=10**6, bytes_accessed=2 * 10**6, transcendentals=0),
        name="prep",
    )(beam_index, beam_taps)


def smooth_kernel(
    index_ref, before, top, bottom, after, col_ref, row_ref, order_ref, out_ref, hi_ref, mid_ref, sm_ref
):
    group = pl.program_id(0)
    columns = before.shape[2]
    blocks = columns // 256
    tiles = columns // 128
    lane = lax.broadcasted_iota(jnp.int32, (128, 128), 1)

    def keep(tile, piece):
        hi, mid = split2(piece)
        for place in range(4):
            rows = slice(place * 32, place * 32 + 32)
            hi_ref[place, tile] = hi[rows]
            mid_ref[place, tile] = mid[rows]

    def row_step(n, tail):
        cols = pl.ds(pl.multiple_of(n * 256, 256), 256)
        data = jnp.concatenate(
            [ref[place, :, cols] for place in range(4) for ref in (before, top, bottom, after)],
            axis=0,
        )
        full = jnp.dot(row_ref[0], data, preferred_element_type=F32)
        value = full[0:128] + full[128:256] + full[256:384]
        moved = pltpu.roll(value, 64, 1)
        keep(2 * n, jnp.where(lane < 64, tail, moved[:, 0:128]))
        keep(2 * n + 1, moved[:, 128:256])
        return moved[:, 0:128]

    tail = lax.fori_loop(0, blocks, row_step, jnp.zeros((128, 128), F32), unroll=ROW_UNROLL)
    keep(tiles, jnp.where(lane < 64, tail, 0.0))

    def col_step(place, carry):
        channel = group * 4 + place
        band = col_ref[index_ref[channel]]
        rows = pl.ds(pl.multiple_of(channel * 32, 32), 32)
        for start in range(0, tiles, COL_RUN):
            total = None
            for ref in (hi_ref, mid_ref):
                data = jnp.concatenate(
                    [
                        ref[place, start : start + COL_RUN].reshape(COL_RUN * 32, 128),
                        ref[place, start + 1 : start + COL_RUN + 1].reshape(COL_RUN * 32, 128),
                    ],
                    axis=1,
                )
                term = lax.dot_general(data, band, NT, preferred_element_type=F32)
                total = term if total is None else total + term
            value = (total[:, 0:128] + total[:, 128:256]).astype(BF16)
            sm_ref[start : start + COL_RUN, rows, :] = value.reshape(COL_RUN, 32, 128)
        return carry

    lax.fori_loop(0, 4, col_step, 0, unroll=COL_UNROLL)

    @pl.when(group == pl.num_programs(0) - 1)
    def _():
        channels = out_ref.shape[1]
        lane3 = lax.broadcasted_iota(jnp.int32, (12, channels, 128), 2)

        def place_step(n, carry):
            data = jnp.concatenate([sm_ref[2 * n], sm_ref[2 * n + 1]], axis=1)
            moved = jnp.dot(order_ref[...], data, preferred_element_type=F32)
            for t in range(2):
                four = moved[:, t * 128 : t * 128 + 128].reshape(12, 2, channels, 128)
                even, odd = four[:, 0], four[:, 1]
                low = jnp.where(lane3 < 64, even, pltpu.roll(odd, 64, 2)).astype(BF16)
                high = jnp.where(lane3 < 64, pltpu.roll(even, 64, 2), odd).astype(BF16)
                for q in range(12):
                    out_ref[4 * n + 2 * t, :, q * 128 : q * 128 + 128] = low[q]
                    out_ref[4 * n + 2 * t + 1, :, q * 128 : q * 128 + 128] = high[q]
            return carry

        lax.fori_loop(0, blocks, place_step, 0, unroll=PLACE_UNROLL)


def smooth(beam_index, before, top, bottom, after, col, row, order):
    channels, _, columns = before.shape
    tiles = columns // 128
    strip = pl.BlockSpec((4, 16, columns), lambda g: (g, 0, 0))
    return pl.pallas_call(
        smooth_kernel,
        grid=(channels // 4,),
        out_shape=jax.ShapeDtypeStruct((columns // 64, channels, 1536), BF16),
        in_specs=[smem()]
        + [strip] * 4
        + [
            pl.BlockSpec(col.shape, lambda g: (0, 0, 0)),
            pl.BlockSpec((1,) + row.shape[1:], lambda g: (g, 0, 0)),
            pl.BlockSpec(order.shape, lambda g: (0, 0)),
        ],
        out_specs=pl.BlockSpec((columns // 64, channels, 1536), lambda g: (0, 0, 0)),
        scratch_shapes=[
            pltpu.VMEM((4, tiles + 1, 32, 128), BF16),
            pltpu.VMEM((4, tiles + 1, 32, 128), BF16),
            pltpu.VMEM((tiles, channels * 32, 128), BF16),
        ],
        compiler_params=pltpu.CompilerParams(vmem_limit_bytes=VMEM_LIMIT),
        cost_estimate=pl.CostEstimate(
            flops=5 * 10**8 * channels, bytes_accessed=10**6 * channels, transcendentals=0
        ),
        name="smooth",
    )(beam_index, before, top, bottom, after, col, row, order)


def load_parts(parts, data_ref, sems):
    copies, first = [], 0
    for k, part in enumerate(parts):
        rows = part.shape[0]
        copies.append(
            pltpu.make_async_copy(part, data_ref.at[first : first + rows], sems.at[k])
        )
        first += rows
    for copy in copies:
        copy.start()
    return copies


def cov_kernel(core_ref, part0, part1, keep_ref, send_ref, data_ref, sems):
    for copy in load_parts((part0, part1, part0), data_ref, sems):
        copy.wait()
    core = core_ref[0]

    def fill(out_ref, first):
        for unit in range(2):
            start = pl.multiple_of((first + 2 * unit) * 128, 256)
            wide = lax.dot_general(
                data_ref[pl.ds(start, 768), :],
                data_ref[pl.ds(start, 256), :],
                NT,
                preferred_element_type=F32,
            ).astype(out_ref.dtype)
            out_ref[2 * unit] = wide[0:640, 0:128]
            out_ref[2 * unit + 1] = wide[128:768, 128:256]

    fill(keep_ref, core * 4)
    fill(send_ref, (1 - core) * 4)


def anywhere():
    return pl.BlockSpec(memory_space=pl.ANY)


def local_covariance(core, parts):
    rows = sum(part.shape[0] for part in parts)
    return pl.pallas_call(
        cov_kernel,
        out_shape=(
            jax.ShapeDtypeStruct((4, 640, 128), F32),
            jax.ShapeDtypeStruct((4, 640, 128), BF16),
        ),
        in_specs=[smem(), anywhere(), anywhere()],
        out_specs=(vmem(), vmem()),
        scratch_shapes=[
            pltpu.VMEM((rows + parts[0].shape[0], parts[0].shape[1]), BF16),
            pltpu.SemaphoreType.DMA((3,)),
        ],
        compiler_params=pltpu.CompilerParams(vmem_limit_bytes=VMEM_LIMIT),
        cost_estimate=pl.CostEstimate(
            flops=2 * 10**9, bytes_accessed=6 * 10**6, transcendentals=0
        ),
        name="cov",
    )(core, *parts)


def everywhere(x, axes, size):
    copies = jnp.broadcast_to(x[None], (size,) + x.shape)
    return lax.all_to_all(copies, axes, 0, 0, tiled=True)


def reduce_all(keep, send):
    swap = [(0, 1), (1, 0)]
    half = (keep + lax.ppermute(send, "core", swap).astype(F32)).astype(BF16)
    got = lax.all_to_all(half.reshape(4, 640, 128), "sky", 0, 0, tiled=True)
    quarter = jnp.sum(got.astype(F32), axis=0).astype(BF16)
    got = lax.all_to_all(quarter.reshape(32, 20, 128), ("y", "z"), 0, 0, tiled=True)
    mine = jnp.sum(got.astype(F32), axis=0)
    quarter = everywhere(mine, ("y", "z"), 32).reshape(640, 128)
    half = everywhere(quarter, "sky", 4).reshape(4, 640, 128)
    other = lax.ppermute(half, "core", swap)
    return half, other


def start_factor(gram):
    size = gram.shape[0]
    row = lax.broadcasted_iota(jnp.int32, (size, 128), 0)
    lane = lax.broadcasted_iota(jnp.int32, (size, 128), 1)
    unit = jnp.where(lane == row, 1.0, 0.0).astype(F32)
    columns = [jnp.broadcast_to(gram[:, j : j + 1], (size, 128)) for j in range(size)]
    return columns + [unit, jnp.ones((size, 128), F32)]


def eliminate(work, j):
    size = len(work) - 2
    shape = work[0].shape
    row = lax.broadcasted_iota(jnp.int32, shape, 0)
    pivot = jnp.broadcast_to(work[j][j : j + 1, :], shape)
    factor = jnp.where(row > j, work[j], 0.0) * (1.0 / pivot)
    new = list(work)
    for k in list(range(j + 1, size)) + [size]:
        new[k] = work[k] - factor * jnp.broadcast_to(work[k][j : j + 1, :], shape)
    new[size + 1] = jnp.where(row == j, pivot, work[size + 1])
    return new


def end_factor(work):
    inverse, pivot = work[-2], work[-1]
    size = inverse.shape[0]
    scale = lax.rsqrt(pivot)
    scale = scale * (1.5 - 0.5 * pivot * scale * scale)
    return (inverse * scale)[:, 0:size]


def clean_kernel(
    core_ref, near_ref, far_ref, seed_ref, part0, part1, out_ref, data_ref, cov_ref, basis_ref, coef_ref, sems
):
    core = core_ref[0]
    copies = load_parts((part0, part1), data_ref, sems)
    modes = seed_ref.shape[0] // 3
    count = seed_ref.shape[1]
    pixels = data_ref.shape[1]
    scale = 1.0 / (256 * pixels)
    for i in range(8):
        for d in range(5):
            rows = slice(d * 128, d * 128 + 128)
            near, far = near_ref[i % 4, rows, :], far_ref[i % 4, rows, :]
            block = jnp.where(core == i // 4, near, far) * scale
            j = (i + d) % 8
            hi, mid = split2(block)
            cov_ref[j * 128 : j * 128 + 128, i * 256 : i * 256 + 128] = hi
            cov_ref[j * 128 : j * 128 + 128, i * 256 + 128 : i * 256 + 256] = mid
            if d in (1, 2, 3):
                hi, mid = split2(block.T)
                cov_ref[i * 128 : i * 128 + 128, j * 256 : j * 256 + 128] = hi
                cov_ref[i * 128 : i * 128 + 128, j * 256 + 128 : j * 256 + 256] = mid

    def fold(x):
        return x[0:modes] + x[modes : 2 * modes] + x[2 * modes : 3 * modes]

    def stack(x):
        return jnp.concatenate(split3(x), axis=0)

    def cov_block(parts, q):
        wide = fold(
            jnp.dot(parts, cov_ref[:, q * 256 : q * 256 + 256], preferred_element_type=F32)
        )
        return wide[:, 0:128] + wide[:, 128:256]

    def gram_of(parts):
        tall = fold(lax.dot_general(parts, parts, NT, preferred_element_type=F32))
        return tall[:, 0:modes] + tall[:, modes : 2 * modes] + tall[:, 2 * modes : 3 * modes]

    def exact_dot(a, b):
        return lax.dot(a, b, precision=lax.Precision.HIGHEST, preferred_element_type=F32)

    seeds = seed_ref[...]
    images = jnp.concatenate([cov_block(seeds, q) for q in range(8)], axis=1)

    def sweep(step, images):
        parts = stack(images)
        work = start_factor(gram_of(parts))
        blocks = []
        for q in range(8):
            blocks.append(cov_block(parts, q))
            work = eliminate(eliminate(work, 2 * q), 2 * q + 1)
        return exact_dot(end_factor(work), jnp.concatenate(blocks, axis=1))

    images = lax.fori_loop(0, ITERS - 1, sweep, images)
    work = start_factor(gram_of(stack(images)))
    for j in range(modes):
        work = eliminate(work, j)
    basis = exact_dot(end_factor(work), images)
    hi, mid, low = split3(basis)
    basis_ref[...] = jnp.concatenate([hi, hi, mid, mid, hi, low], axis=0)
    for copy in copies:
        copy.wait()
    data = data_ref[...]
    coef = fold(
        jnp.dot(jnp.concatenate([hi, mid, low], axis=0), data, preferred_element_type=F32)
    )
    hi, mid, low = split3(coef)
    coef_ref[...] = jnp.concatenate([hi, mid, hi, mid, low, hi], axis=0)
    for m in range(count // 128):
        rows = slice(m * 128, m * 128 + 128)
        part = lax.dot_general(
            basis_ref[:, rows], coef_ref[...], TN, preferred_element_type=F32
        )
        value = (data_ref[rows, :].astype(F32) - part).astype(BF16)
        chunk, first = m // 4, (m % 4) * 16
        out_ref[first : first + 16, chunk * 8 : chunk * 8 + 8, :] = value.reshape(16, 8, pixels)


def seeds_kernel(seed_ref, out_ref):
    out_ref[...] = jnp.concatenate(split3(seed_ref[...].astype(F32)), axis=0)


def split_seed(seed):
    modes, count = seed.shape
    return pl.pallas_call(
        seeds_kernel,
        out_shape=jax.ShapeDtypeStruct((3 * modes, count), BF16),
        in_specs=[vmem()],
        out_specs=vmem(),
        name="seeds",
    )(seed)


def clean(core, near, far, seed, parts):
    modes, count = seed.shape
    modes = modes // 3
    pixels = parts[0].shape[1]
    return pl.pallas_call(
        clean_kernel,
        out_shape=jax.ShapeDtypeStruct((count // 16, 16, pixels), BF16),
        in_specs=[smem()] + [vmem()] * 3 + [anywhere(), anywhere()],
        out_specs=vmem(),
        scratch_shapes=[
            pltpu.VMEM((count, pixels), BF16),
            pltpu.VMEM((count, 2 * count), BF16),
            pltpu.VMEM((6 * modes, count), BF16),
            pltpu.VMEM((6 * modes, pixels), BF16),
            pltpu.SemaphoreType.DMA((2,)),
        ],
        compiler_params=pltpu.CompilerParams(vmem_limit_bytes=VMEM_LIMIT),
        cost_estimate=pl.CostEstimate(
            flops=3 * 10**9, bytes_accessed=12 * 10**6, transcendentals=0
        ),
        name="clean",
    )(core, near, far, seed, *parts)


def body(sky_maps, beam_index, beam_taps, start_seed):
    channels, strip_rows, _ = sky_maps.shape
    modes = start_seed.shape[1]
    core = lax.axis_index("core").astype(jnp.int32).reshape(1)
    col, row, order = prepare(beam_index, beam_taps, CHUNK)
    halos = []
    for first in range(0, channels, CHUNK):
        strip = sky_maps if first == 0 else lax.optimization_barrier(sky_maps)
        strip = strip[first : first + CHUNK]
        top = strip[:, 0:16, :]
        bottom = strip[:, strip_rows - 16 : strip_rows, :]
        k = first // CHUNK
        before = lax.ppermute(bottom, "sky", [(i, i + 1) for i in range(3)])
        after = lax.ppermute(top, "sky", [(i + 1, i) for i in range(3)])
        halos.append((before, top, bottom, after))
    parts = []
    for k, halo in enumerate(halos):
        mine = slice(k * CHUNK, (k + 1) * CHUNK)
        rows = row[k * CHUNK // 4 : (k + 1) * CHUNK // 4]
        pieces = smooth(beam_index[mine], *halo, col, rows, order)
        data = lax.all_to_all(pieces, ("y", "z", "core"), 0, 0, tiled=True)
        parts.append(data.reshape(64 * CHUNK, 1536))
    seed = start_seed.T.reshape(modes, 64, channels // CHUNK, CHUNK)
    seed = seed.transpose(0, 2, 1, 3).reshape(modes, 64 * channels)
    seed = split_seed(seed)
    keep, send = local_covariance(core, parts)
    near, far = reduce_all(keep, send)
    cleaned = clean(core, near, far, seed, parts)
    return cleaned.reshape(64 * channels, 1, 1536)


def solution(mesh):
    fine = Mesh(mesh.devices.reshape(4, 8, 2, 4), ("y", "z", "core", "sky"))
    freq = ("y", "z", "core")

    return jax.shard_map(
        body,
        mesh=fine,
        in_specs=(P(freq, "sky", None), P(freq), P(), P()),
        out_specs=P(None, freq + ("sky",), None),
        check_vma=False,
    )
```

```python
import jax
import jax.numpy as jnp
from jax import lax
from jax.experimental import pallas as pl
from jax.experimental.pallas import tpu as pltpu
from jax.sharding import Mesh, PartitionSpec as P


ITERS = 8
F32 = jnp.float32
BF16 = jnp.bfloat16
NT = (((1,), (1,)), ((), ()))
TN = (((0,), (0,)), ((), ()))
ROW_UNROLL, COL_UNROLL, PLACE_UNROLL, COL_RUN = 16, 4, 16, 16
CHUNK = 8
VMEM_LIMIT = 20 * 1024 * 1024


def vmem():
    return pl.BlockSpec(memory_space=pltpu.VMEM)


def smem():
    return pl.BlockSpec(memory_space=pltpu.SMEM)


def split2(x):
    hi = x.astype(BF16)
    return hi, (x - hi.astype(F32)).astype(BF16)


def split3(x):
    hi = x.astype(BF16)
    rest = x - hi.astype(F32)
    mid = rest.astype(BF16)
    return hi, mid, (rest - mid.astype(F32)).astype(BF16)


def prep_kernel(index_ref, taps_ref, col_ref, row_ref, order_ref, padded_ref):
    beams, taps = taps_ref.shape
    channels = index_ref.shape[0]
    padded_ref[...] = jnp.zeros_like(padded_ref)
    padded_ref[:, 0:taps] = taps_ref[...]
    table = padded_ref[...]
    table = table / jnp.sum(table, axis=1, keepdims=True)
    padded_ref[...] = table
    for beam in range(beams):
        line = jnp.broadcast_to(table[beam : beam + 1, :], (128, 256))
        band = pltpu.roll(line, 49, 1, stride=1, stride_axis=0)
        hi, mid = split2(band)
        col_ref[beam, 0:128, :] = hi
        col_ref[beam, 128:256, :] = mid
    lane = lax.broadcasted_iota(jnp.int32, (32, 256), 1)
    line_no = lax.broadcasted_iota(jnp.int32, (32, 256), 0)
    for channel in range(channels):
        line = jnp.broadcast_to(padded_ref[pl.ds(index_ref[channel], 1), :], (32, 256))
        band = pltpu.roll(line, 1, 1, stride=1, stride_axis=0)
        moved = pltpu.roll(band, 8, 1)
        band = jnp.where(lane < 32, band, jnp.where(lane < 40, 0.0, moved))
        band = jnp.where((lane < 64) & (line_no < 24), band, 0.0)
        group, place = channel // 4, channel % 4
        if place:
            band = pltpu.roll(band, 64 * place, 1)
        for part, value in enumerate(split3(band)):
            row_ref[group, part * 128 + place * 32 : part * 128 + place * 32 + 32, :] = value
    rows = order_ref.shape[0]
    out_row = lax.broadcasted_iota(jnp.int32, order_ref.shape, 0)
    in_row = lax.broadcasted_iota(jnp.int32, order_ref.shape, 1)
    count = rows // 24
    wanted = (out_row % count) * 32 + out_row // count
    order_ref[...] = jnp.where(in_row == wanted, 1.0, 0.0).astype(BF16)


def prepare(beam_index, beam_taps, chunk):
    channels = beam_index.shape[0]
    beams = beam_taps.shape[0]
    return pl.pallas_call(
        prep_kernel,
        out_shape=(
            jax.ShapeDtypeStruct((beams, 256, 256), BF16),
            jax.ShapeDtypeStruct((channels // 4, 384, 256), BF16),
            jax.ShapeDtypeStruct((chunk * 24, chunk * 32), BF16),
        ),
        in_specs=[smem(), vmem()],
        out_specs=(vmem(), vmem(), vmem()),
        scratch_shapes=[pltpu.VMEM((beams, 256), F32)],
        cost_estimate=pl.CostEstimate(flops=10**6, bytes_accessed=2 * 10**6, transcendentals=0),
        name="prep",
    )(beam_index, beam_taps)


def smooth_kernel(
    index_ref, before, top, bottom, after, col_ref, row_ref, order_ref, out_ref, hi_ref, mid_ref, sm_ref
):
    group = pl.program_id(0)
    columns = before.shape[2]
    blocks = columns // 256
    tiles = columns // 128
    lane = lax.broadcasted_iota(jnp.int32, (128, 128), 1)

    def keep(tile, piece):
        hi, mid = split2(piece)
        for place in range(4):
            rows = slice(place * 32, place * 32 + 32)
            hi_ref[place, tile] = hi[rows]
            mid_ref[place, tile] = mid[rows]

    def row_step(n, tail):
        cols = pl.ds(pl.multiple_of(n * 256, 256), 256)
        data = jnp.concatenate(
            [ref[place, :, cols] for place in range(4) for ref in (before, top, bottom, after)],
            axis=0,
        )
        full = jnp.dot(row_ref[0], data, preferred_element_type=F32)
        value = full[0:128] + full[128:256] + full[256:384]
        moved = pltpu.roll(value, 64, 1)
        keep(2 * n, jnp.where(lane < 64, tail, moved[:, 0:128]))
        keep(2 * n + 1, moved[:, 128:256])
        return moved[:, 0:128]

    tail = lax.fori_loop(0, blocks, row_step, jnp.zeros((128, 128), F32), unroll=ROW_UNROLL)
    keep(tiles, jnp.where(lane < 64, tail, 0.0))

    def col_step(place, carry):
        channel = group * 4 + place
        band = col_ref[index_ref[channel]]
        rows = pl.ds(pl.multiple_of(channel * 32, 32), 32)
        for start in range(0, tiles, COL_RUN):
            total = None
            for ref in (hi_ref, mid_ref):
                data = jnp.concatenate(
                    [
                        ref[place, start : start + COL_RUN].reshape(COL_RUN * 32, 128),
                        ref[place, start + 1 : start + COL_RUN + 1].reshape(COL_RUN * 32, 128),
                    ],
                    axis=1,
                )
                term = lax.dot_general(data, band, NT, preferred_element_type=F32)
                total = term if total is None else total + term
            value = (total[:, 0:128] + total[:, 128:256]).astype(BF16)
            sm_ref[start : start + COL_RUN, rows, :] = value.reshape(COL_RUN, 32, 128)
        return carry

    lax.fori_loop(0, 4, col_step, 0, unroll=COL_UNROLL)

    @pl.when(group == pl.num_programs(0) - 1)
    def _():
        channels = out_ref.shape[1]
        lane3 = lax.broadcasted_iota(jnp.int32, (12, channels, 128), 2)

        def place_step(n, carry):
            data = jnp.concatenate([sm_ref[2 * n], sm_ref[2 * n + 1]], axis=1)
            moved = jnp.dot(order_ref[...], data, preferred_element_type=F32)
            for t in range(2):
                four = moved[:, t * 128 : t * 128 + 128].reshape(12, 2, channels, 128)
                even, odd = four[:, 0], four[:, 1]
                low = jnp.where(lane3 < 64, even, pltpu.roll(odd, 64, 2)).astype(BF16)
                high = jnp.where(lane3 < 64, pltpu.roll(even, 64, 2), odd).astype(BF16)
                for q in range(12):
                    out_ref[4 * n + 2 * t, :, q * 128 : q * 128 + 128] = low[q]
                    out_ref[4 * n + 2 * t + 1, :, q * 128 : q * 128 + 128] = high[q]
            return carry

        lax.fori_loop(0, blocks, place_step, 0, unroll=PLACE_UNROLL)


def smooth(beam_index, before, top, bottom, after, col, row, order):
    channels, _, columns = before.shape
    tiles = columns // 128
    strip = pl.BlockSpec((4, 16, columns), lambda g: (g, 0, 0))
    return pl.pallas_call(
        smooth_kernel,
        grid=(channels // 4,),
        out_shape=jax.ShapeDtypeStruct((columns // 64, channels, 1536), BF16),
        in_specs=[smem()]
        + [strip] * 4
        + [
            pl.BlockSpec(col.shape, lambda g: (0, 0, 0)),
            pl.BlockSpec((1,) + row.shape[1:], lambda g: (g, 0, 0)),
            pl.BlockSpec(order.shape, lambda g: (0, 0)),
        ],
        out_specs=pl.BlockSpec((columns // 64, channels, 1536), lambda g: (0, 0, 0)),
        scratch_shapes=[
            pltpu.VMEM((4, tiles + 1, 32, 128), BF16),
            pltpu.VMEM((4, tiles + 1, 32, 128), BF16),
            pltpu.VMEM((tiles, channels * 32, 128), BF16),
        ],
        compiler_params=pltpu.CompilerParams(vmem_limit_bytes=VMEM_LIMIT),
        cost_estimate=pl.CostEstimate(
            flops=5 * 10**8 * channels, bytes_accessed=10**6 * channels, transcendentals=0
        ),
        name="smooth",
    )(beam_index, before, top, bottom, after, col, row, order)


def load_parts(parts, data_ref, sems):
    copies, first = [], 0
    for k, part in enumerate(parts):
        rows = part.shape[0]
        copies.append(
            pltpu.make_async_copy(part, data_ref.at[first : first + rows], sems.at[k])
        )
        first += rows
    for copy in copies:
        copy.start()
    return copies


def cov_kernel(core_ref, part0, part1, keep_ref, send_ref, data_ref, sems):
    for copy in load_parts((part0, part1, part0), data_ref, sems):
        copy.wait()
    core = core_ref[0]

    def fill(out_ref, first):
        for unit in range(2):
            start = pl.multiple_of((first + 2 * unit) * 128, 256)
            wide = lax.dot_general(
                data_ref[pl.ds(start, 768), :],
                data_ref[pl.ds(start, 256), :],
                NT,
                preferred_element_type=F32,
            ).astype(out_ref.dtype)
            out_ref[2 * unit] = wide[0:640, 0:128]
            out_ref[2 * unit + 1] = wide[128:768, 128:256]

    fill(keep_ref, core * 4)
    fill(send_ref, (1 - core) * 4)


def anywhere():
    return pl.BlockSpec(memory_space=pl.ANY)


def local_covariance(core, parts):
    rows = sum(part.shape[0] for part in parts)
    return pl.pallas_call(
        cov_kernel,
        out_shape=(
            jax.ShapeDtypeStruct((4, 640, 128), F32),
            jax.ShapeDtypeStruct((4, 640, 128), BF16),
        ),
        in_specs=[smem(), anywhere(), anywhere()],
        out_specs=(vmem(), vmem()),
        scratch_shapes=[
            pltpu.VMEM((rows + parts[0].shape[0], parts[0].shape[1]), BF16),
            pltpu.SemaphoreType.DMA((3,)),
        ],
        compiler_params=pltpu.CompilerParams(vmem_limit_bytes=VMEM_LIMIT),
        cost_estimate=pl.CostEstimate(
            flops=2 * 10**9, bytes_accessed=6 * 10**6, transcendentals=0
        ),
        name="cov",
    )(core, *parts)


def everywhere(x, axes, size):
    copies = jnp.broadcast_to(x[None], (size,) + x.shape)
    return lax.all_to_all(copies, axes, 0, 0, tiled=True)


def reduce_all(keep, send):
    swap = [(0, 1), (1, 0)]
    half = (keep + lax.ppermute(send, "core", swap).astype(F32)).astype(BF16)
    got = lax.all_to_all(half.reshape(4, 640, 128), "sky", 0, 0, tiled=True)
    quarter = jnp.sum(got.astype(F32), axis=0).astype(BF16)
    got = lax.all_to_all(quarter.reshape(32, 20, 128), ("y", "z"), 0, 0, tiled=True)
    mine = jnp.sum(got.astype(F32), axis=0)
    quarter = everywhere(mine, ("y", "z"), 32).reshape(640, 128)
    half = everywhere(quarter, "sky", 4).reshape(4, 640, 128)
    other = lax.ppermute(half, "core", swap)
    return half, other


def start_factor(gram):
    size = gram.shape[0]
    row = lax.broadcasted_iota(jnp.int32, (size, 128), 0)
    lane = lax.broadcasted_iota(jnp.int32, (size, 128), 1)
    unit = jnp.where(lane == row, 1.0, 0.0).astype(F32)
    columns = [jnp.broadcast_to(gram[:, j : j + 1], (size, 128)) for j in range(size)]
    return columns + [unit, jnp.ones((size, 128), F32)]


def eliminate(work, j):
    size = len(work) - 2
    shape = work[0].shape
    row = lax.broadcasted_iota(jnp.int32, shape, 0)
    pivot = jnp.broadcast_to(work[j][j : j + 1, :], shape)
    factor = jnp.where(row > j, work[j], 0.0) * (1.0 / pivot)
    new = list(work)
    for k in list(range(j + 1, size)) + [size]:
        new[k] = work[k] - factor * jnp.broadcast_to(work[k][j : j + 1, :], shape)
    new[size + 1] = jnp.where(row == j, pivot, work[size + 1])
    return new


def end_factor(work):
    inverse, pivot = work[-2], work[-1]
    size = inverse.shape[0]
    scale = lax.rsqrt(pivot)
    scale = scale * (1.5 - 0.5 * pivot * scale * scale)
    return (inverse * scale)[:, 0:size]


def clean_kernel(
    core_ref, near_ref, far_ref, seed_ref, part0, part1, out_ref, data_ref, cov_ref, basis_ref, coef_ref, done_ref, sems, out_sems
):
    core = core_ref[0]
    copies = load_parts((part0, part1), data_ref, sems)
    modes = seed_ref.shape[0] // 3
    count = seed_ref.shape[1]
    pixels = data_ref.shape[1]
    scale = 1.0 / (256 * pixels)
    for i in range(8):
        for d in range(5):
            rows = slice(d * 128, d * 128 + 128)
            near, far = near_ref[i % 4, rows, :], far_ref[i % 4, rows, :]
            block = jnp.where(core == i // 4, near, far) * scale
            j = (i + d) % 8
            hi, mid = split2(block)
            cov_ref[j * 128 : j * 128 + 128, i * 256 : i * 256 + 128] = hi
            cov_ref[j * 128 : j * 128 + 128, i * 256 + 128 : i * 256 + 256] = mid
            if d in (1, 2, 3):
                hi, mid = split2(block.T)
                cov_ref[i * 128 : i * 128 + 128, j * 256 : j * 256 + 128] = hi
                cov_ref[i * 128 : i * 128 + 128, j * 256 + 128 : j * 256 + 256] = mid

    def fold(x):
        return x[0:modes] + x[modes : 2 * modes] + x[2 * modes : 3 * modes]

    def stack(x):
        return jnp.concatenate(split3(x), axis=0)

    def cov_block(parts, q):
        wide = fold(
            jnp.dot(parts, cov_ref[:, q * 256 : q * 256 + 256], preferred_element_type=F32)
        )
        return wide[:, 0:128] + wide[:, 128:256]

    def gram_of(parts):
        tall = fold(lax.dot_general(parts, parts, NT, preferred_element_type=F32))
        return tall[:, 0:modes] + tall[:, modes : 2 * modes] + tall[:, 2 * modes : 3 * modes]

    def exact_dot(a, b):
        return lax.dot(a, b, precision=lax.Precision.HIGHEST, preferred_element_type=F32)

    seeds = seed_ref[...]
    images = jnp.concatenate([cov_block(seeds, q) for q in range(8)], axis=1)

    def sweep(step, images):
        parts = stack(images)
        work = start_factor(gram_of(parts))
        blocks = []
        for q in range(8):
            blocks.append(cov_block(parts, q))
            work = eliminate(eliminate(work, 2 * q), 2 * q + 1)
        return exact_dot(end_factor(work), jnp.concatenate(blocks, axis=1))

    images = lax.fori_loop(0, ITERS - 1, sweep, images)
    work = start_factor(gram_of(stack(images)))
    for j in range(modes):
        work = eliminate(work, j)
    basis = exact_dot(end_factor(work), images)
    hi, mid, low = split3(basis)
    basis_ref[...] = jnp.concatenate([hi, hi, mid, mid, hi, low], axis=0)
    for copy in copies:
        copy.wait()
    data = data_ref[...]
    coef = fold(
        jnp.dot(jnp.concatenate([hi, mid, low], axis=0), data, preferred_element_type=F32)
    )
    hi, mid, low = split3(coef)
    coef_ref[...] = jnp.concatenate([hi, mid, hi, mid, low, hi], axis=0)
    sent = []
    for m in range(count // 128):
        rows = slice(m * 128, m * 128 + 128)
        part = lax.dot_general(
            basis_ref[:, rows], coef_ref[...], TN, preferred_element_type=F32
        )
        value = (data_ref[rows, :].astype(F32) - part).astype(BF16)
        chunk, first = m // 4, (m % 4) * 16
        done_ref[m] = value.reshape(16, 8, pixels)
        copy = pltpu.make_async_copy(
            done_ref.at[m],
            out_ref.at[first : first + 16, chunk * 8 : chunk * 8 + 8, :],
            out_sems.at[m],
        )
        copy.start()
        sent.append(copy)
    for copy in sent:
        copy.wait()


def seeds_kernel(seed_ref, out_ref):
    out_ref[...] = jnp.concatenate(split3(seed_ref[...].astype(F32)), axis=0)


def split_seed(seed):
    modes, count = seed.shape
    return pl.pallas_call(
        seeds_kernel,
        out_shape=jax.ShapeDtypeStruct((3 * modes, count), BF16),
        in_specs=[vmem()],
        out_specs=vmem(),
        name="seeds",
    )(seed)


def clean(core, near, far, seed, parts):
    modes, count = seed.shape
    modes = modes // 3
    pixels = parts[0].shape[1]
    return pl.pallas_call(
        clean_kernel,
        out_shape=jax.ShapeDtypeStruct((count // 16, 16, pixels), BF16),
        in_specs=[smem()] + [vmem()] * 3 + [anywhere(), anywhere()],
        out_specs=anywhere(),
        scratch_shapes=[
            pltpu.VMEM((count, pixels), BF16),
            pltpu.VMEM((count, 2 * count), BF16),
            pltpu.VMEM((6 * modes, count), BF16),
            pltpu.VMEM((6 * modes, pixels), BF16),
            pltpu.VMEM((count // 128, 16, 8, pixels), BF16),
            pltpu.SemaphoreType.DMA((2,)),
            pltpu.SemaphoreType.DMA((count // 128,)),
        ],
        compiler_params=pltpu.CompilerParams(vmem_limit_bytes=VMEM_LIMIT),
        cost_estimate=pl.CostEstimate(
            flops=3 * 10**9, bytes_accessed=12 * 10**6, transcendentals=0
        ),
        name="clean",
    )(core, near, far, seed, *parts)


def body(sky_maps, beam_index, beam_taps, start_seed):
    channels, strip_rows, _ = sky_maps.shape
    modes = start_seed.shape[1]
    core = lax.axis_index("core").astype(jnp.int32).reshape(1)
    col, row, order = prepare(beam_index, beam_taps, CHUNK)
    halos = []
    for first in range(0, channels, CHUNK):
        strip = sky_maps if first == 0 else lax.optimization_barrier(sky_maps)
        strip = strip[first : first + CHUNK]
        top = strip[:, 0:16, :]
        bottom = strip[:, strip_rows - 16 : strip_rows, :]
        k = first // CHUNK
        before = lax.ppermute(bottom, "sky", [(i, i + 1) for i in range(3)])
        after = lax.ppermute(top, "sky", [(i + 1, i) for i in range(3)])
        halos.append((before, top, bottom, after))
    parts = []
    for k, halo in enumerate(halos):
        mine = slice(k * CHUNK, (k + 1) * CHUNK)
        rows = row[k * CHUNK // 4 : (k + 1) * CHUNK // 4]
        pieces = smooth(beam_index[mine], *halo, col, rows, order)
        data = lax.all_to_all(pieces, ("y", "z", "core"), 0, 0, tiled=True)
        parts.append(data.reshape(64 * CHUNK, 1536))
    seed = start_seed.T.reshape(modes, 64, channels // CHUNK, CHUNK)
    seed = seed.transpose(0, 2, 1, 3).reshape(modes, 64 * channels)
    seed = split_seed(seed)
    keep, send = local_covariance(core, parts)
    near, far = reduce_all(keep, send)
    cleaned = clean(core, near, far, seed, parts)
    return cleaned.reshape(64 * channels, 1, 1536)


def solution(mesh):
    fine = Mesh(mesh.devices.reshape(4, 8, 2, 4), ("y", "z", "core", "sky"))
    freq = ("y", "z", "core")

    return jax.shard_map(
        body,
        mesh=fine,
        in_specs=(P(freq, "sky", None), P(freq), P(), P()),
        out_specs=P(None, freq + ("sky",), None),
        check_vma=False,
    )
```

```python
import jax
import jax.numpy as jnp
from jax import lax
from jax.experimental import pallas as pl
from jax.experimental.pallas import tpu as pltpu
from jax.sharding import Mesh, PartitionSpec as P


ITERS = 8
F32 = jnp.float32
BF16 = jnp.bfloat16
NT = (((1,), (1,)), ((), ()))
TN = (((0,), (0,)), ((), ()))
ROW_UNROLL, COL_UNROLL, PLACE_UNROLL, COL_RUN = 16, 4, 16, 16
CHUNK = 8
VMEM_LIMIT = 20 * 1024 * 1024


def vmem():
    return pl.BlockSpec(memory_space=pltpu.VMEM)


def smem():
    return pl.BlockSpec(memory_space=pltpu.SMEM)


def split2(x):
    hi = x.astype(BF16)
    return hi, (x - hi.astype(F32)).astype(BF16)


def split3(x):
    hi = x.astype(BF16)
    rest = x - hi.astype(F32)
    mid = rest.astype(BF16)
    return hi, mid, (rest - mid.astype(F32)).astype(BF16)


def prep_kernel(index_ref, taps_ref, col_ref, row_ref, order_ref, padded_ref):
    beams, taps = taps_ref.shape
    channels = index_ref.shape[0]
    padded_ref[...] = jnp.zeros_like(padded_ref)
    padded_ref[:, 0:taps] = taps_ref[...]
    table = padded_ref[...]
    table = table / jnp.sum(table, axis=1, keepdims=True)
    padded_ref[...] = table
    for beam in range(beams):
        line = jnp.broadcast_to(table[beam : beam + 1, :], (128, 256))
        band = pltpu.roll(line, 49, 1, stride=1, stride_axis=0)
        hi, mid = split2(band)
        col_ref[beam, 0:128, :] = hi
        col_ref[beam, 128:256, :] = mid
    lane = lax.broadcasted_iota(jnp.int32, (32, 256), 1)
    line_no = lax.broadcasted_iota(jnp.int32, (32, 256), 0)
    for channel in range(channels):
        line = jnp.broadcast_to(padded_ref[pl.ds(index_ref[channel], 1), :], (32, 256))
        band = pltpu.roll(line, 1, 1, stride=1, stride_axis=0)
        moved = pltpu.roll(band, 8, 1)
        band = jnp.where(lane < 32, band, jnp.where(lane < 40, 0.0, moved))
        band = jnp.where((lane < 64) & (line_no < 24), band, 0.0)
        group, place = channel // 4, channel % 4
        if place:
            band = pltpu.roll(band, 64 * place, 1)
        for part, value in enumerate(split3(band)):
            row_ref[group, part * 128 + place * 32 : part * 128 + place * 32 + 32, :] = value
    rows = order_ref.shape[0]
    out_row = lax.broadcasted_iota(jnp.int32, order_ref.shape, 0)
    in_row = lax.broadcasted_iota(jnp.int32, order_ref.shape, 1)
    count = rows // 24
    wanted = (out_row % count) * 32 + out_row // count
    order_ref[...] = jnp.where(in_row == wanted, 1.0, 0.0).astype(BF16)


def prepare(beam_index, beam_taps, chunk):
    channels = beam_index.shape[0]
    beams = beam_taps.shape[0]
    return pl.pallas_call(
        prep_kernel,
        out_shape=(
            jax.ShapeDtypeStruct((beams, 256, 256), BF16),
            jax.ShapeDtypeStruct((channels // 4, 384, 256), BF16),
            jax.ShapeDtypeStruct((chunk * 24, chunk * 32), BF16),
        ),
        in_specs=[smem(), vmem()],
        out_specs=(vmem(), vmem(), vmem()),
        scratch_shapes=[pltpu.VMEM((beams, 256), F32)],
        cost_estimate=pl.CostEstimate(flops=10**6, bytes_accessed=2 * 10**6, transcendentals=0),
        name="prep",
    )(beam_index, beam_taps)


def smooth_group(group, index_ref, strips, col_ref, row_ref, hi_ref, mid_ref, sm_ref):
    columns = strips[0].shape[2]
    blocks = columns // 256
    tiles = columns // 128
    lane = lax.broadcasted_iota(jnp.int32, (128, 128), 1)

    def keep(tile, piece):
        hi, mid = split2(piece)
        for place in range(4):
            rows = slice(place * 32, place * 32 + 32)
            hi_ref[place, tile] = hi[rows]
            mid_ref[place, tile] = mid[rows]

    def row_step(n, tail):
        cols = pl.ds(pl.multiple_of(n * 256, 256), 256)
        data = jnp.concatenate(
            [ref[place, :, cols] for place in range(4) for ref in strips], axis=0
        )
        full = jnp.dot(row_ref[0], data, preferred_element_type=F32)
        value = full[0:128] + full[128:256] + full[256:384]
        moved = pltpu.roll(value, 64, 1)
        keep(2 * n, jnp.where(lane < 64, tail, moved[:, 0:128]))
        keep(2 * n + 1, moved[:, 128:256])
        return moved[:, 0:128]

    tail = lax.fori_loop(0, blocks, row_step, jnp.zeros((128, 128), F32), unroll=ROW_UNROLL)
    keep(tiles, jnp.where(lane < 64, tail, 0.0))

    def col_step(place, carry):
        channel = group * 4 + place
        band = col_ref[index_ref[channel]]
        rows = pl.ds(pl.multiple_of(channel * 32, 32), 32)
        for start in range(0, tiles, COL_RUN):
            total = None
            for ref in (hi_ref, mid_ref):
                data = jnp.concatenate(
                    [
                        ref[place, start : start + COL_RUN].reshape(COL_RUN * 32, 128),
                        ref[place, start + 1 : start + COL_RUN + 1].reshape(COL_RUN * 32, 128),
                    ],
                    axis=1,
                )
                term = lax.dot_general(data, band, NT, preferred_element_type=F32)
                total = term if total is None else total + term
            value = (total[:, 0:128] + total[:, 128:256]).astype(BF16)
            sm_ref[start : start + COL_RUN, rows, :] = value.reshape(COL_RUN, 32, 128)
        return carry

    lax.fori_loop(0, 4, col_step, 0, unroll=COL_UNROLL)


def place_tiles(sm_refs, order_ref, out_ref):
    channels = out_ref.shape[1]
    lane3 = lax.broadcasted_iota(jnp.int32, (12, channels, 128), 2)

    def place_step(n, carry):
        data = jnp.concatenate(
            [
                jnp.concatenate([ref[2 * n + t] for ref in sm_refs], axis=0)
                for t in range(2)
            ],
            axis=1,
        )
        moved = jnp.dot(order_ref[...], data, preferred_element_type=F32)
        for t in range(2):
            four = moved[:, t * 128 : t * 128 + 128].reshape(12, 2, channels, 128)
            even, odd = four[:, 0], four[:, 1]
            low = jnp.where(lane3 < 64, even, pltpu.roll(odd, 64, 2)).astype(BF16)
            high = jnp.where(lane3 < 64, pltpu.roll(even, 64, 2), odd).astype(BF16)
            for q in range(12):
                out_ref[4 * n + 2 * t, :, q * 128 : q * 128 + 128] = low[q]
                out_ref[4 * n + 2 * t + 1, :, q * 128 : q * 128 + 128] = high[q]
        return carry

    lax.fori_loop(0, out_ref.shape[0] // 4, place_step, 0, unroll=PLACE_UNROLL)


def smooth_kernel(
    index_ref, before, top, bottom, after, col_ref, row_ref, order_ref, out_ref, hi_ref, mid_ref, sm_ref
):
    group = pl.program_id(0)
    strips = (before, top, bottom, after)
    smooth_group(group, index_ref, strips, col_ref, row_ref, hi_ref, mid_ref, sm_ref)

    @pl.when(group == pl.num_programs(0) - 1)
    def _():
        place_tiles((sm_ref,), order_ref, out_ref)


def first_kernel(
    index_ref, before, top, bottom, after, col_ref, row_ref, sm_ref, hi_ref, mid_ref
):
    strips = (before, top, bottom, after)
    smooth_group(0, index_ref, strips, col_ref, row_ref, hi_ref, mid_ref, sm_ref)


def second_kernel(
    index_ref, before, top, bottom, after, col_ref, row_ref, first_ref, order_ref, out_ref, hi_ref, mid_ref, sm_ref
):
    strips = (before, top, bottom, after)
    smooth_group(0, index_ref, strips, col_ref, row_ref, hi_ref, mid_ref, sm_ref)
    place_tiles((first_ref, sm_ref), order_ref, out_ref)


def smooth_cost(channels):
    return pl.CostEstimate(
        flops=5 * 10**8 * channels, bytes_accessed=10**6 * channels, transcendentals=0
    )


def half_scratch(tiles):
    return [pltpu.VMEM((4, tiles + 1, 32, 128), BF16)] * 2


def smooth_first(beam_index, halo, col, row):
    tiles = halo[0].shape[2] // 128
    return pl.pallas_call(
        first_kernel,
        out_shape=jax.ShapeDtypeStruct((tiles, 128, 128), BF16),
        in_specs=[smem()] + [vmem()] * 6,
        out_specs=vmem(),
        scratch_shapes=half_scratch(tiles),
        compiler_params=pltpu.CompilerParams(vmem_limit_bytes=VMEM_LIMIT),
        cost_estimate=smooth_cost(4),
        name="first",
    )(beam_index, *halo, col, row)


def smooth_second(beam_index, halo, col, row, first, order):
    columns = halo[0].shape[2]
    tiles = columns // 128
    return pl.pallas_call(
        second_kernel,
        out_shape=jax.ShapeDtypeStruct((columns // 64, 8, 1536), BF16),
        in_specs=[smem()] + [vmem()] * 8,
        out_specs=vmem(),
        scratch_shapes=half_scratch(tiles) + [pltpu.VMEM((tiles, 128, 128), BF16)],
        compiler_params=pltpu.CompilerParams(vmem_limit_bytes=VMEM_LIMIT),
        cost_estimate=smooth_cost(4),
        name="second",
    )(beam_index, *halo, col, row, first, order)


def smooth(beam_index, before, top, bottom, after, col, row, order):
    channels, _, columns = before.shape
    tiles = columns // 128
    strip = pl.BlockSpec((4, 16, columns), lambda g: (g, 0, 0))
    return pl.pallas_call(
        smooth_kernel,
        grid=(channels // 4,),
        out_shape=jax.ShapeDtypeStruct((columns // 64, channels, 1536), BF16),
        in_specs=[smem()]
        + [strip] * 4
        + [
            pl.BlockSpec(col.shape, lambda g: (0, 0, 0)),
            pl.BlockSpec((1,) + row.shape[1:], lambda g: (g, 0, 0)),
            pl.BlockSpec(order.shape, lambda g: (0, 0)),
        ],
        out_specs=pl.BlockSpec((columns // 64, channels, 1536), lambda g: (0, 0, 0)),
        scratch_shapes=half_scratch(tiles) + [pltpu.VMEM((tiles, channels * 32, 128), BF16)],
        compiler_params=pltpu.CompilerParams(vmem_limit_bytes=VMEM_LIMIT),
        cost_estimate=smooth_cost(channels),
        name="smooth",
    )(beam_index, before, top, bottom, after, col, row, order)


def load_parts(parts, data_ref, sems):
    copies, first = [], 0
    for k, part in enumerate(parts):
        rows = part.shape[0]
        copies.append(
            pltpu.make_async_copy(part, data_ref.at[first : first + rows], sems.at[k])
        )
        first += rows
    for copy in copies:
        copy.start()
    return copies


def cov_kernel(core_ref, part0, part1, keep_ref, send_ref, tiles_ref, data_ref, sems, tiles_sem):
    for copy in load_parts((part0, part1, part0), data_ref, sems):
        copy.wait()
    tiles_copy = pltpu.make_async_copy(
        data_ref.at[0 : tiles_ref.shape[0]], tiles_ref, tiles_sem
    )
    tiles_copy.start()
    core = core_ref[0]

    def fill(out_ref, first):
        for unit in range(2):
            start = pl.multiple_of((first + 2 * unit) * 128, 256)
            wide = lax.dot_general(
                data_ref[pl.ds(start, 768), :],
                data_ref[pl.ds(start, 256), :],
                NT,
                preferred_element_type=F32,
            ).astype(out_ref.dtype)
            out_ref[2 * unit] = wide[0:640, 0:128]
            out_ref[2 * unit + 1] = wide[128:768, 128:256]

    fill(keep_ref, core * 4)
    fill(send_ref, (1 - core) * 4)
    tiles_copy.wait()


def anywhere():
    return pl.BlockSpec(memory_space=pl.ANY)


def local_covariance(core, parts):
    rows = sum(part.shape[0] for part in parts)
    return pl.pallas_call(
        cov_kernel,
        out_shape=(
            jax.ShapeDtypeStruct((4, 640, 128), F32),
            jax.ShapeDtypeStruct((4, 640, 128), BF16),
            jax.ShapeDtypeStruct((rows, parts[0].shape[1]), BF16),
        ),
        in_specs=[smem(), anywhere(), anywhere()],
        out_specs=(vmem(), vmem(), pl.BlockSpec(memory_space=pltpu.HBM)),
        scratch_shapes=[
            pltpu.VMEM((rows + parts[0].shape[0], parts[0].shape[1]), BF16),
            pltpu.SemaphoreType.DMA((3,)),
            pltpu.SemaphoreType.DMA,
        ],
        compiler_params=pltpu.CompilerParams(vmem_limit_bytes=VMEM_LIMIT),
        cost_estimate=pl.CostEstimate(
            flops=2 * 10**9, bytes_accessed=6 * 10**6, transcendentals=0
        ),
        name="cov",
    )(core, *parts)


def everywhere(x, axes, size):
    copies = jnp.broadcast_to(x[None], (size,) + x.shape)
    return lax.all_to_all(copies, axes, 0, 0, tiled=True)


def reduce_all(keep, send):
    swap = [(0, 1), (1, 0)]
    half = (keep + lax.ppermute(send, "core", swap).astype(F32)).astype(BF16)
    half = half.reshape(4, 640, 128)
    sky = lax.axis_index("sky")
    total = lax.dynamic_index_in_dim(half, sky, 0, False).astype(F32)
    for d in (2, 1, 3):
        block = lax.dynamic_index_in_dim(half, lax.rem(sky + d, 4), 0, False)
        total += lax.ppermute(block, "sky", [(i, (i + d) % 4) for i in range(4)]).astype(F32)
    quarter = total.astype(BF16)
    got = lax.all_to_all(quarter.reshape(32, 20, 128), ("y", "z"), 0, 0, tiled=True)
    mine = jnp.sum(got.astype(F32), axis=0)
    quarter = everywhere(mine, ("y", "z"), 32).reshape(640, 128)
    half = everywhere(quarter, "sky", 4).reshape(4, 640, 128)
    other = lax.ppermute(half, "core", swap)
    return half, other


def start_factor(gram):
    size = gram.shape[0]
    row = lax.broadcasted_iota(jnp.int32, (size, 128), 0)
    lane = lax.broadcasted_iota(jnp.int32, (size, 128), 1)
    unit = jnp.where(lane == row, 1.0, 0.0).astype(F32)
    columns = [jnp.broadcast_to(gram[:, j : j + 1], (size, 128)) for j in range(size)]
    return columns + [unit, jnp.ones((size, 128), F32)]


def eliminate(work, j):
    size = len(work) - 2
    shape = work[0].shape
    row = lax.broadcasted_iota(jnp.int32, shape, 0)
    pivot = jnp.broadcast_to(work[j][j : j + 1, :], shape)
    factor = jnp.where(row > j, work[j], 0.0) * (1.0 / pivot)
    new = list(work)
    for k in list(range(j + 1, size)) + [size]:
        new[k] = work[k] - factor * jnp.broadcast_to(work[k][j : j + 1, :], shape)
    new[size + 1] = jnp.where(row == j, pivot, work[size + 1])
    return new


def end_factor(work):
    inverse, pivot = work[-2], work[-1]
    size = inverse.shape[0]
    scale = lax.rsqrt(pivot)
    scale = scale * (1.5 - 0.5 * pivot * scale * scale)
    return (inverse * scale)[:, 0:size]


def clean_kernel(
    core_ref, near_ref, far_ref, seed_ref, tiles_ref, out_ref, data_ref, cov_ref, basis_ref, coef_ref, done_ref, sem, out_sems
):
    core = core_ref[0]
    tiles_copy = pltpu.make_async_copy(tiles_ref, data_ref, sem)
    tiles_copy.start()
    modes = seed_ref.shape[0] // 3
    count = seed_ref.shape[1]
    pixels = data_ref.shape[1]
    scale = 1.0 / (256 * pixels)
    for i in range(8):
        for d in range(5):
            rows = slice(d * 128, d * 128 + 128)
            near, far = near_ref[i % 4, rows, :], far_ref[i % 4, rows, :]
            block = jnp.where(core == i // 4, near, far) * scale
            j = (i + d) % 8
            hi, mid = split2(block)
            cov_ref[j * 128 : j * 128 + 128, i * 256 : i * 256 + 128] = hi
            cov_ref[j * 128 : j * 128 + 128, i * 256 + 128 : i * 256 + 256] = mid
            if d in (1, 2, 3):
                hi, mid = split2(block.T)
                cov_ref[i * 128 : i * 128 + 128, j * 256 : j * 256 + 128] = hi
                cov_ref[i * 128 : i * 128 + 128, j * 256 + 128 : j * 256 + 256] = mid

    def fold(x):
        return x[0:modes] + x[modes : 2 * modes] + x[2 * modes : 3 * modes]

    def stack(x):
        return jnp.concatenate(split3(x), axis=0)

    def cov_block(parts, q):
        wide = fold(
            jnp.dot(parts, cov_ref[:, q * 256 : q * 256 + 256], preferred_element_type=F32)
        )
        return wide[:, 0:128] + wide[:, 128:256]

    def gram_of(parts):
        tall = fold(lax.dot_general(parts, parts, NT, preferred_element_type=F32))
        return tall[:, 0:modes] + tall[:, modes : 2 * modes] + tall[:, 2 * modes : 3 * modes]

    def exact_dot(a, b):
        return lax.dot(a, b, precision=lax.Precision.HIGHEST, preferred_element_type=F32)

    seeds = seed_ref[...]
    images = jnp.concatenate([cov_block(seeds, q) for q in range(8)], axis=1)

    def sweep(step, images):
        parts = stack(images)
        work = start_factor(gram_of(parts))
        blocks = []
        for q in range(8):
            blocks.append(cov_block(parts, q))
            work = eliminate(eliminate(work, 2 * q), 2 * q + 1)
        return exact_dot(end_factor(work), jnp.concatenate(blocks, axis=1))

    images = lax.fori_loop(0, ITERS - 1, sweep, images)
    work = start_factor(gram_of(stack(images)))
    for j in range(modes):
        work = eliminate(work, j)
    basis = exact_dot(end_factor(work), images)
    hi, mid, low = split3(basis)
    basis_ref[...] = jnp.concatenate([hi, hi, mid, mid, hi, low], axis=0)
    tiles_copy.wait()
    data = data_ref[...]
    coef = fold(
        jnp.dot(jnp.concatenate([hi, mid, low], axis=0), data, preferred_element_type=F32)
    )
    hi, mid, low = split3(coef)
    coef_ref[...] = jnp.concatenate([hi, mid, hi, mid, low, hi], axis=0)
    sent = []
    for m in range(count // 128):
        rows = slice(m * 128, m * 128 + 128)
        part = lax.dot_general(
            basis_ref[:, rows], coef_ref[...], TN, preferred_element_type=F32
        )
        value = (data_ref[rows, :].astype(F32) - part).astype(BF16)
        chunk, first = m // 4, (m % 4) * 16
        done_ref[m] = value.reshape(16, 8, pixels)
        copy = pltpu.make_async_copy(
            done_ref.at[m],
            out_ref.at[first : first + 16, chunk * 8 : chunk * 8 + 8, :],
            out_sems.at[m],
        )
        copy.start()
        sent.append(copy)
    for copy in sent:
        copy.wait()


def seeds_kernel(seed_ref, out_ref):
    out_ref[...] = jnp.concatenate(split3(seed_ref[...].astype(F32)), axis=0)


def split_seed(seed):
    modes, count = seed.shape
    return pl.pallas_call(
        seeds_kernel,
        out_shape=jax.ShapeDtypeStruct((3 * modes, count), BF16),
        in_specs=[vmem()],
        out_specs=vmem(),
        name="seeds",
    )(seed)


def clean(core, near, far, seed, tiles):
    modes, count = seed.shape
    modes = modes // 3
    pixels = tiles.shape[1]
    return pl.pallas_call(
        clean_kernel,
        out_shape=jax.ShapeDtypeStruct((count // 16, 16, pixels), BF16),
        in_specs=[smem()] + [vmem()] * 3 + [pl.BlockSpec(memory_space=pltpu.HBM)],
        out_specs=anywhere(),
        scratch_shapes=[
            pltpu.VMEM((count, pixels), BF16),
            pltpu.VMEM((count, 2 * count), BF16),
            pltpu.VMEM((6 * modes, count), BF16),
            pltpu.VMEM((6 * modes, pixels), BF16),
            pltpu.VMEM((count // 128, 16, 8, pixels), BF16),
            pltpu.SemaphoreType.DMA,
            pltpu.SemaphoreType.DMA((count // 128,)),
        ],
        compiler_params=pltpu.CompilerParams(vmem_limit_bytes=VMEM_LIMIT),
        cost_estimate=pl.CostEstimate(
            flops=3 * 10**9, bytes_accessed=12 * 10**6, transcendentals=0
        ),
        name="clean",
    )(core, near, far, seed, tiles)


def body(sky_maps, beam_index, beam_taps, start_seed):
    channels, strip_rows, _ = sky_maps.shape
    modes = start_seed.shape[1]
    core = lax.axis_index("core").astype(jnp.int32).reshape(1)
    col, row, order = prepare(beam_index, beam_taps, CHUNK)
    halos = []
    for first, last in ((0, 4), (4, 8), (8, 16)):
        strip = sky_maps if first == 0 else lax.optimization_barrier(sky_maps)
        strip = strip[first:last]
        top = strip[:, 0:16, :]
        bottom = strip[:, strip_rows - 16 : strip_rows, :]
        before = lax.ppermute(bottom, "sky", [(i, i + 1) for i in range(3)])
        after = lax.ppermute(top, "sky", [(i + 1, i) for i in range(3)])
        halos.append((before, top, bottom, after))
    first = smooth_first(beam_index[0:4], halos[0], col, row[0:1])
    pieces0 = smooth_second(beam_index[4:8], halos[1], col, row[1:2], first, order)
    pieces1 = smooth(beam_index[8:16], *halos[2], col, row[2:4], order)
    parts = []
    for pieces in (pieces0, pieces1):
        data = lax.all_to_all(pieces, ("y", "z", "core"), 0, 0, tiled=True)
        parts.append(data.reshape(64 * CHUNK, 1536))
    seed = start_seed.T.reshape(modes, 64, channels // CHUNK, CHUNK)
    seed = seed.transpose(0, 2, 1, 3).reshape(modes, 64 * channels)
    seed = split_seed(seed)
    keep, send, tiles = local_covariance(core, parts)
    near, far = reduce_all(keep, send)
    cleaned = clean(core, near, far, seed, tiles)
    return cleaned.reshape(64 * channels, 1, 1536)


def solution(mesh):
    fine = Mesh(mesh.devices.reshape(4, 8, 2, 4), ("y", "z", "core", "sky"))
    freq = ("y", "z", "core")

    return jax.shard_map(
        body,
        mesh=fine,
        in_specs=(P(freq, "sky", None), P(freq), P(), P()),
        out_specs=P(None, freq + ("sky",), None),
        check_vma=False,
    )
```

```python
import jax
import jax.numpy as jnp
from jax import lax
from jax.experimental import pallas as pl
from jax.experimental.pallas import tpu as pltpu
from jax.sharding import Mesh, PartitionSpec as P


ITERS = 8
F32 = jnp.float32
BF16 = jnp.bfloat16
NT = (((1,), (1,)), ((), ()))
TN = (((0,), (0,)), ((), ()))
ROW_UNROLL, COL_UNROLL, PLACE_UNROLL, COL_RUN = 16, 4, 16, 16
CHUNK = 8
VMEM_LIMIT = 20 * 1024 * 1024


def vmem():
    return pl.BlockSpec(memory_space=pltpu.VMEM)


def smem():
    return pl.BlockSpec(memory_space=pltpu.SMEM)


def split2(x):
    hi = x.astype(BF16)
    return hi, (x - hi.astype(F32)).astype(BF16)


def split3(x):
    hi = x.astype(BF16)
    rest = x - hi.astype(F32)
    mid = rest.astype(BF16)
    return hi, mid, (rest - mid.astype(F32)).astype(BF16)


def prep_kernel(index_ref, taps_ref, col_ref, row_ref, order_ref, padded_ref):
    beams, taps = taps_ref.shape
    channels = index_ref.shape[0]
    padded_ref[...] = jnp.zeros_like(padded_ref)
    padded_ref[:, 0:taps] = taps_ref[...]
    table = padded_ref[...]
    table = table / jnp.sum(table, axis=1, keepdims=True)
    padded_ref[...] = table
    for beam in range(beams):
        line = jnp.broadcast_to(table[beam : beam + 1, :], (128, 256))
        band = pltpu.roll(line, 49, 1, stride=1, stride_axis=0)
        hi, mid = split2(band)
        col_ref[beam, 0:128, :] = hi
        col_ref[beam, 128:256, :] = mid
    lane = lax.broadcasted_iota(jnp.int32, (32, 256), 1)
    line_no = lax.broadcasted_iota(jnp.int32, (32, 256), 0)
    for channel in range(channels):
        line = jnp.broadcast_to(padded_ref[pl.ds(index_ref[channel], 1), :], (32, 256))
        band = pltpu.roll(line, 1, 1, stride=1, stride_axis=0)
        moved = pltpu.roll(band, 8, 1)
        band = jnp.where(lane < 32, band, jnp.where(lane < 40, 0.0, moved))
        band = jnp.where((lane < 64) & (line_no < 24), band, 0.0)
        group, place = channel // 4, channel % 4
        if place:
            band = pltpu.roll(band, 64 * place, 1)
        for part, value in enumerate(split3(band)):
            row_ref[group, part * 128 + place * 32 : part * 128 + place * 32 + 32, :] = value
    rows = order_ref.shape[0]
    out_row = lax.broadcasted_iota(jnp.int32, order_ref.shape, 0)
    in_row = lax.broadcasted_iota(jnp.int32, order_ref.shape, 1)
    count = rows // 24
    wanted = (out_row % count) * 32 + out_row // count
    order_ref[...] = jnp.where(in_row == wanted, 1.0, 0.0).astype(BF16)


def prepare(beam_index, beam_taps, chunk):
    channels = beam_index.shape[0]
    beams = beam_taps.shape[0]
    return pl.pallas_call(
        prep_kernel,
        out_shape=(
            jax.ShapeDtypeStruct((beams, 256, 256), BF16),
            jax.ShapeDtypeStruct((channels // 4, 384, 256), BF16),
            jax.ShapeDtypeStruct((chunk * 24, chunk * 32), BF16),
        ),
        in_specs=[smem(), vmem()],
        out_specs=(vmem(), vmem(), vmem()),
        scratch_shapes=[pltpu.VMEM((beams, 256), F32)],
        cost_estimate=pl.CostEstimate(flops=10**6, bytes_accessed=2 * 10**6, transcendentals=0),
        name="prep",
    )(beam_index, beam_taps)


def smooth_group(group, index_ref, strips, col_ref, row_ref, hi_ref, mid_ref, sm_ref):
    columns = strips[0].shape[2]
    blocks = columns // 256
    tiles = columns // 128
    lane = lax.broadcasted_iota(jnp.int32, (128, 128), 1)

    def keep(tile, piece):
        hi, mid = split2(piece)
        for place in range(4):
            rows = slice(place * 32, place * 32 + 32)
            hi_ref[place, tile] = hi[rows]
            mid_ref[place, tile] = mid[rows]

    def row_step(n, tail):
        cols = pl.ds(pl.multiple_of(n * 256, 256), 256)
        data = jnp.concatenate(
            [ref[place, :, cols] for place in range(4) for ref in strips], axis=0
        )
        full = jnp.dot(row_ref[0], data, preferred_element_type=F32)
        value = full[0:128] + full[128:256] + full[256:384]
        moved = pltpu.roll(value, 64, 1)
        keep(2 * n, jnp.where(lane < 64, tail, moved[:, 0:128]))
        keep(2 * n + 1, moved[:, 128:256])
        return moved[:, 0:128]

    tail = lax.fori_loop(0, blocks, row_step, jnp.zeros((128, 128), F32), unroll=ROW_UNROLL)
    keep(tiles, jnp.where(lane < 64, tail, 0.0))

    def col_step(place, carry):
        channel = group * 4 + place
        band = col_ref[index_ref[channel]]
        rows = pl.ds(pl.multiple_of(channel * 32, 32), 32)
        for start in range(0, tiles, COL_RUN):
            total = None
            for ref in (hi_ref, mid_ref):
                data = jnp.concatenate(
                    [
                        ref[place, start : start + COL_RUN].reshape(COL_RUN * 32, 128),
                        ref[place, start + 1 : start + COL_RUN + 1].reshape(COL_RUN * 32, 128),
                    ],
                    axis=1,
                )
                term = lax.dot_general(data, band, NT, preferred_element_type=F32)
                total = term if total is None else total + term
            value = (total[:, 0:128] + total[:, 128:256]).astype(BF16)
            sm_ref[start : start + COL_RUN, rows, :] = value.reshape(COL_RUN, 32, 128)
        return carry

    lax.fori_loop(0, 4, col_step, 0, unroll=COL_UNROLL)


def place_tiles(sm_refs, order_ref, out_ref):
    channels = out_ref.shape[1]
    lane3 = lax.broadcasted_iota(jnp.int32, (12, channels, 128), 2)

    def place_step(n, carry):
        data = jnp.concatenate(
            [
                jnp.concatenate([ref[2 * n + t] for ref in sm_refs], axis=0)
                for t in range(2)
            ],
            axis=1,
        )
        moved = jnp.dot(order_ref[...], data, preferred_element_type=F32)
        for t in range(2):
            four = moved[:, t * 128 : t * 128 + 128].reshape(12, 2, channels, 128)
            even, odd = four[:, 0], four[:, 1]
            low = jnp.where(lane3 < 64, even, pltpu.roll(odd, 64, 2)).astype(BF16)
            high = jnp.where(lane3 < 64, pltpu.roll(even, 64, 2), odd).astype(BF16)
            for q in range(12):
                out_ref[4 * n + 2 * t, :, q * 128 : q * 128 + 128] = low[q]
                out_ref[4 * n + 2 * t + 1, :, q * 128 : q * 128 + 128] = high[q]
        return carry

    lax.fori_loop(0, out_ref.shape[0] // 4, place_step, 0, unroll=PLACE_UNROLL)


def smooth_kernel(
    index_ref, before, top, bottom, after, col_ref, row_ref, order_ref, out_ref, hi_ref, mid_ref, sm_ref
):
    group = pl.program_id(0)
    strips = (before, top, bottom, after)
    smooth_group(group, index_ref, strips, col_ref, row_ref, hi_ref, mid_ref, sm_ref)

    @pl.when(group == pl.num_programs(0) - 1)
    def _():
        place_tiles((sm_ref,), order_ref, out_ref)


def first_kernel(
    index_ref, before, top, bottom, after, col_ref, row_ref, sm_ref, hi_ref, mid_ref
):
    strips = (before, top, bottom, after)
    smooth_group(0, index_ref, strips, col_ref, row_ref, hi_ref, mid_ref, sm_ref)


def second_kernel(
    index_ref, before, top, bottom, after, col_ref, row_ref, first_ref, order_ref, out_ref, hi_ref, mid_ref, sm_ref
):
    strips = (before, top, bottom, after)
    smooth_group(0, index_ref, strips, col_ref, row_ref, hi_ref, mid_ref, sm_ref)
    place_tiles((first_ref, sm_ref), order_ref, out_ref)


def smooth_cost(channels):
    return pl.CostEstimate(
        flops=5 * 10**8 * channels, bytes_accessed=10**6 * channels, transcendentals=0
    )


def half_scratch(tiles):
    return [pltpu.VMEM((4, tiles + 1, 32, 128), BF16)] * 2


def smooth_first(beam_index, halo, col, row):
    tiles = halo[0].shape[2] // 128
    return pl.pallas_call(
        first_kernel,
        out_shape=jax.ShapeDtypeStruct((tiles, 128, 128), BF16),
        in_specs=[smem()] + [vmem()] * 6,
        out_specs=vmem(),
        scratch_shapes=half_scratch(tiles),
        compiler_params=pltpu.CompilerParams(vmem_limit_bytes=VMEM_LIMIT),
        cost_estimate=smooth_cost(4),
        name="first",
    )(beam_index, *halo, col, row)


def smooth_second(beam_index, halo, col, row, first, order):
    columns = halo[0].shape[2]
    tiles = columns // 128
    return pl.pallas_call(
        second_kernel,
        out_shape=jax.ShapeDtypeStruct((columns // 64, 8, 1536), BF16),
        in_specs=[smem()] + [vmem()] * 8,
        out_specs=vmem(),
        scratch_shapes=half_scratch(tiles) + [pltpu.VMEM((tiles, 128, 128), BF16)],
        compiler_params=pltpu.CompilerParams(vmem_limit_bytes=VMEM_LIMIT),
        cost_estimate=smooth_cost(4),
        name="second",
    )(beam_index, *halo, col, row, first, order)


def smooth(beam_index, before, top, bottom, after, col, row, order):
    channels, _, columns = before.shape
    tiles = columns // 128
    strip = pl.BlockSpec((4, 16, columns), lambda g: (g, 0, 0))
    return pl.pallas_call(
        smooth_kernel,
        grid=(channels // 4,),
        out_shape=jax.ShapeDtypeStruct((columns // 64, channels, 1536), BF16),
        in_specs=[smem()]
        + [strip] * 4
        + [
            pl.BlockSpec(col.shape, lambda g: (0, 0, 0)),
            pl.BlockSpec((1,) + row.shape[1:], lambda g: (g, 0, 0)),
            pl.BlockSpec(order.shape, lambda g: (0, 0)),
        ],
        out_specs=pl.BlockSpec((columns // 64, channels, 1536), lambda g: (0, 0, 0)),
        scratch_shapes=half_scratch(tiles) + [pltpu.VMEM((tiles, channels * 32, 128), BF16)],
        compiler_params=pltpu.CompilerParams(vmem_limit_bytes=VMEM_LIMIT),
        cost_estimate=smooth_cost(channels),
        name="smooth",
    )(beam_index, before, top, bottom, after, col, row, order)


def load_parts(parts, data_ref, sems):
    copies, first = [], 0
    for k, part in enumerate(parts):
        rows = part.shape[0]
        copies.append(
            pltpu.make_async_copy(part, data_ref.at[first : first + rows], sems.at[k])
        )
        first += rows
    for copy in copies:
        copy.start()
    return copies


def cov_kernel(core_ref, part0, part1, keep_ref, send_ref, tiles_ref, data_ref, sems, tiles_sem):
    for copy in load_parts((part0, part1, part0), data_ref, sems):
        copy.wait()
    rows = part0.shape[0] + part1.shape[0]
    tiles_copy = pltpu.make_async_copy(
        data_ref.at[0:rows], tiles_ref.at[0:rows], tiles_sem
    )
    tiles_copy.start()
    core = core_ref[0]

    def fill(out_ref, first):
        for unit in range(2):
            start = pl.multiple_of((first + 2 * unit) * 128, 256)
            wide = lax.dot_general(
                data_ref[pl.ds(start, 768), :],
                data_ref[pl.ds(start, 256), :],
                NT,
                preferred_element_type=F32,
            ).astype(out_ref.dtype)
            out_ref[2 * unit] = wide[0:640, 0:128]
            out_ref[2 * unit + 1] = wide[128:768, 128:256]

    fill(keep_ref, core * 4)
    fill(send_ref, (1 - core) * 4)
    tiles_copy.wait()


def anywhere():
    return pl.BlockSpec(memory_space=pl.ANY)


def local_covariance(core, parts):
    rows = sum(part.shape[0] for part in parts)
    return pl.pallas_call(
        cov_kernel,
        out_shape=(
            jax.ShapeDtypeStruct((4, 640, 128), F32),
            jax.ShapeDtypeStruct((4, 640, 128), BF16),
            jax.ShapeDtypeStruct((8 * rows, parts[0].shape[1]), BF16),
        ),
        in_specs=[smem(), anywhere(), anywhere()],
        out_specs=(vmem(), vmem(), pl.BlockSpec(memory_space=pltpu.HBM)),
        scratch_shapes=[
            pltpu.VMEM((rows + parts[0].shape[0], parts[0].shape[1]), BF16),
            pltpu.SemaphoreType.DMA((3,)),
            pltpu.SemaphoreType.DMA,
        ],
        compiler_params=pltpu.CompilerParams(vmem_limit_bytes=48 * 1024 * 1024),
        cost_estimate=pl.CostEstimate(
            flops=2 * 10**9, bytes_accessed=6 * 10**6, transcendentals=0
        ),
        name="cov",
    )(core, *parts)


def everywhere(x, axes, size):
    copies = jnp.broadcast_to(x[None], (size,) + x.shape)
    return lax.all_to_all(copies, axes, 0, 0, tiled=True)


def reduce_all(keep, send):
    swap = [(0, 1), (1, 0)]
    half = (keep + lax.ppermute(send, "core", swap).astype(F32)).astype(BF16)
    got = lax.all_to_all(half.reshape(4, 640, 128), "sky", 0, 0, tiled=True)
    quarter = jnp.sum(got.astype(F32), axis=0).astype(BF16)
    got = lax.all_to_all(quarter.reshape(32, 20, 128), ("y", "z"), 0, 0, tiled=True)
    mine = jnp.sum(got.astype(F32), axis=0)
    quarter = everywhere(mine, ("y", "z"), 32).reshape(640, 128)
    half = everywhere(quarter, "sky", 4).reshape(4, 640, 128)
    other = lax.ppermute(half, "core", swap)
    return half, other


def start_factor(gram):
    size = gram.shape[0]
    row = lax.broadcasted_iota(jnp.int32, (size, 128), 0)
    lane = lax.broadcasted_iota(jnp.int32, (size, 128), 1)
    unit = jnp.where(lane == row, 1.0, 0.0).astype(F32)
    columns = [jnp.broadcast_to(gram[:, j : j + 1], (size, 128)) for j in range(size)]
    return columns + [unit, jnp.ones((size, 128), F32)]


def eliminate(work, j):
    size = len(work) - 2
    shape = work[0].shape
    row = lax.broadcasted_iota(jnp.int32, shape, 0)
    pivot = jnp.broadcast_to(work[j][j : j + 1, :], shape)
    factor = jnp.where(row > j, work[j], 0.0) * (1.0 / pivot)
    new = list(work)
    for k in list(range(j + 1, size)) + [size]:
        new[k] = work[k] - factor * jnp.broadcast_to(work[k][j : j + 1, :], shape)
    new[size + 1] = jnp.where(row == j, pivot, work[size + 1])
    return new


def end_factor(work):
    inverse, pivot = work[-2], work[-1]
    size = inverse.shape[0]
    scale = lax.rsqrt(pivot)
    scale = scale * (1.5 - 0.5 * pivot * scale * scale)
    return (inverse * scale)[:, 0:size]


def clean_kernel(
    core_ref, near_ref, far_ref, seed_ref, tiles_ref, out_ref, data_ref, cov_ref, basis_ref, coef_ref, done_ref, sem, out_sems
):
    core = core_ref[0]
    modes = seed_ref.shape[0] // 3
    count = seed_ref.shape[1]
    tiles_copy = pltpu.make_async_copy(tiles_ref.at[0:count], data_ref, sem)
    tiles_copy.start()
    pixels = data_ref.shape[1]
    scale = 1.0 / (256 * pixels)
    for i in range(8):
        for d in range(5):
            rows = slice(d * 128, d * 128 + 128)
            near, far = near_ref[i % 4, rows, :], far_ref[i % 4, rows, :]
            block = jnp.where(core == i // 4, near, far) * scale
            j = (i + d) % 8
            hi, mid = split2(block)
            cov_ref[j * 128 : j * 128 + 128, i * 256 : i * 256 + 128] = hi
            cov_ref[j * 128 : j * 128 + 128, i * 256 + 128 : i * 256 + 256] = mid
            if d in (1, 2, 3):
                hi, mid = split2(block.T)
                cov_ref[i * 128 : i * 128 + 128, j * 256 : j * 256 + 128] = hi
                cov_ref[i * 128 : i * 128 + 128, j * 256 + 128 : j * 256 + 256] = mid

    def fold(x):
        return x[0:modes] + x[modes : 2 * modes] + x[2 * modes : 3 * modes]

    def stack(x):
        return jnp.concatenate(split3(x), axis=0)

    def cov_block(parts, q):
        wide = fold(
            jnp.dot(parts, cov_ref[:, q * 256 : q * 256 + 256], preferred_element_type=F32)
        )
        return wide[:, 0:128] + wide[:, 128:256]

    def gram_of(parts):
        tall = fold(lax.dot_general(parts, parts, NT, preferred_element_type=F32))
        return tall[:, 0:modes] + tall[:, modes : 2 * modes] + tall[:, 2 * modes : 3 * modes]

    def exact_dot(a, b):
        return lax.dot(a, b, precision=lax.Precision.HIGHEST, preferred_element_type=F32)

    seeds = seed_ref[...]
    images = jnp.concatenate([cov_block(seeds, q) for q in range(8)], axis=1)

    def sweep(step, images):
        parts = stack(images)
        work = start_factor(gram_of(parts))
        blocks = []
        for q in range(8):
            blocks.append(cov_block(parts, q))
            work = eliminate(eliminate(work, 2 * q), 2 * q + 1)
        return exact_dot(end_factor(work), jnp.concatenate(blocks, axis=1))

    images = lax.fori_loop(0, ITERS - 1, sweep, images)
    work = start_factor(gram_of(stack(images)))
    for j in range(modes):
        work = eliminate(work, j)
    basis = exact_dot(end_factor(work), images)
    hi, mid, low = split3(basis)
    basis_ref[...] = jnp.concatenate([hi, hi, mid, mid, hi, low], axis=0)
    tiles_copy.wait()
    data = data_ref[...]
    coef = fold(
        jnp.dot(jnp.concatenate([hi, mid, low], axis=0), data, preferred_element_type=F32)
    )
    hi, mid, low = split3(coef)
    coef_ref[...] = jnp.concatenate([hi, mid, hi, mid, low, hi], axis=0)
    sent = []
    for m in range(count // 128):
        rows = slice(m * 128, m * 128 + 128)
        part = lax.dot_general(
            basis_ref[:, rows], coef_ref[...], TN, preferred_element_type=F32
        )
        value = (data_ref[rows, :].astype(F32) - part).astype(BF16)
        chunk, first = m // 4, (m % 4) * 16
        done_ref[m] = value.reshape(16, 8, pixels)
        copy = pltpu.make_async_copy(
            done_ref.at[m],
            out_ref.at[first : first + 16, chunk * 8 : chunk * 8 + 8, :],
            out_sems.at[m],
        )
        copy.start()
        sent.append(copy)
    for copy in sent:
        copy.wait()


def seeds_kernel(seed_ref, out_ref):
    out_ref[...] = jnp.concatenate(split3(seed_ref[...].astype(F32)), axis=0)


def split_seed(seed):
    modes, count = seed.shape
    return pl.pallas_call(
        seeds_kernel,
        out_shape=jax.ShapeDtypeStruct((3 * modes, count), BF16),
        in_specs=[vmem()],
        out_specs=vmem(),
        name="seeds",
    )(seed)


def clean(core, near, far, seed, tiles):
    modes, count = seed.shape
    modes = modes // 3
    pixels = tiles.shape[1]
    return pl.pallas_call(
        clean_kernel,
        out_shape=jax.ShapeDtypeStruct((count // 16, 16, pixels), BF16),
        in_specs=[smem()] + [vmem()] * 3 + [pl.BlockSpec(memory_space=pltpu.HBM)],
        out_specs=anywhere(),
        scratch_shapes=[
            pltpu.VMEM((count, pixels), BF16),
            pltpu.VMEM((count, 2 * count), BF16),
            pltpu.VMEM((6 * modes, count), BF16),
            pltpu.VMEM((6 * modes, pixels), BF16),
            pltpu.VMEM((count // 128, 16, 8, pixels), BF16),
            pltpu.SemaphoreType.DMA,
            pltpu.SemaphoreType.DMA((count // 128,)),
        ],
        compiler_params=pltpu.CompilerParams(vmem_limit_bytes=VMEM_LIMIT),
        cost_estimate=pl.CostEstimate(
            flops=3 * 10**9, bytes_accessed=12 * 10**6, transcendentals=0
        ),
        name="clean",
    )(core, near, far, seed, tiles)


def body(sky_maps, beam_index, beam_taps, start_seed):
    channels, strip_rows, _ = sky_maps.shape
    modes = start_seed.shape[1]
    core = lax.axis_index("core").astype(jnp.int32).reshape(1)
    col, row, order = prepare(beam_index, beam_taps, CHUNK)
    halos = []
    for first, last in ((0, 4), (4, 8), (8, 16)):
        strip = sky_maps if first == 0 else lax.optimization_barrier(sky_maps)
        strip = strip[first:last]
        top = strip[:, 0:16, :]
        bottom = strip[:, strip_rows - 16 : strip_rows, :]
        before = lax.ppermute(bottom, "sky", [(i, i + 1) for i in range(3)])
        after = lax.ppermute(top, "sky", [(i + 1, i) for i in range(3)])
        halos.append((before, top, bottom, after))
    first = smooth_first(beam_index[0:4], halos[0], col, row[0:1])
    pieces0 = smooth_second(beam_index[4:8], halos[1], col, row[1:2], first, order)
    pieces1 = smooth(beam_index[8:16], *halos[2], col, row[2:4], order)
    parts = []
    for pieces in (pieces0, pieces1):
        data = lax.all_to_all(pieces, ("y", "z", "core"), 0, 0, tiled=True)
        parts.append(data.reshape(64 * CHUNK, 1536))
    seed = start_seed.T.reshape(modes, 64, channels // CHUNK, CHUNK)
    seed = seed.transpose(0, 2, 1, 3).reshape(modes, 64 * channels)
    seed = split_seed(seed)
    keep, send, tiles = local_covariance(core, parts)
    near, far = reduce_all(keep, send)
    cleaned = clean(core, near, far, seed, tiles)
    return cleaned.reshape(64 * channels, 1, 1536)


def solution(mesh):
    fine = Mesh(mesh.devices.reshape(4, 8, 2, 4), ("y", "z", "core", "sky"))
    freq = ("y", "z", "core")

    return jax.shard_map(
        body,
        mesh=fine,
        in_specs=(P(freq, "sky", None), P(freq), P(), P()),
        out_specs=P(None, freq + ("sky",), None),
        check_vma=False,
    )
```

```python
import jax
import jax.numpy as jnp
from jax import lax
from jax.experimental import pallas as pl
from jax.experimental.pallas import tpu as pltpu
from jax.sharding import Mesh, PartitionSpec as P


ITERS = 8
F32 = jnp.float32
BF16 = jnp.bfloat16
NT = (((1,), (1,)), ((), ()))
TN = (((0,), (0,)), ((), ()))
ROW_UNROLL, COL_UNROLL, PLACE_UNROLL, COL_RUN = 16, 4, 16, 16
CHUNK = 8
VMEM_LIMIT = 20 * 1024 * 1024


def vmem():
    return pl.BlockSpec(memory_space=pltpu.VMEM)


def smem():
    return pl.BlockSpec(memory_space=pltpu.SMEM)


def split2(x):
    hi = x.astype(BF16)
    return hi, (x - hi.astype(F32)).astype(BF16)


def split3(x):
    hi = x.astype(BF16)
    rest = x - hi.astype(F32)
    mid = rest.astype(BF16)
    return hi, mid, (rest - mid.astype(F32)).astype(BF16)


def prep_kernel(index_ref, taps_ref, col_ref, row_ref, order_ref, padded_ref):
    beams, taps = taps_ref.shape
    channels = index_ref.shape[0]
    padded_ref[...] = jnp.zeros_like(padded_ref)
    padded_ref[:, 0:taps] = taps_ref[...]
    table = padded_ref[...]
    table = table / jnp.sum(table, axis=1, keepdims=True)
    padded_ref[...] = table
    for beam in range(beams):
        line = jnp.broadcast_to(table[beam : beam + 1, :], (128, 256))
        band = pltpu.roll(line, 49, 1, stride=1, stride_axis=0)
        hi, mid = split2(band)
        col_ref[beam, 0:128, :] = hi
        col_ref[beam, 128:256, :] = mid
    lane = lax.broadcasted_iota(jnp.int32, (32, 256), 1)
    line_no = lax.broadcasted_iota(jnp.int32, (32, 256), 0)
    for channel in range(channels):
        line = jnp.broadcast_to(padded_ref[pl.ds(index_ref[channel], 1), :], (32, 256))
        band = pltpu.roll(line, 1, 1, stride=1, stride_axis=0)
        moved = pltpu.roll(band, 8, 1)
        band = jnp.where(lane < 32, band, jnp.where(lane < 40, 0.0, moved))
        band = jnp.where((lane < 64) & (line_no < 24), band, 0.0)
        group, place = channel // 4, channel % 4
        if place:
            band = pltpu.roll(band, 64 * place, 1)
        for part, value in enumerate(split3(band)):
            row_ref[group, part * 128 + place * 32 : part * 128 + place * 32 + 32, :] = value
    rows = order_ref.shape[0]
    out_row = lax.broadcasted_iota(jnp.int32, order_ref.shape, 0)
    in_row = lax.broadcasted_iota(jnp.int32, order_ref.shape, 1)
    count = rows // 24
    wanted = (out_row % count) * 32 + out_row // count
    order_ref[...] = jnp.where(in_row == wanted, 1.0, 0.0).astype(BF16)


def prepare(beam_index, beam_taps, chunk):
    channels = beam_index.shape[0]
    beams = beam_taps.shape[0]
    return pl.pallas_call(
        prep_kernel,
        out_shape=(
            jax.ShapeDtypeStruct((beams, 256, 256), BF16),
            jax.ShapeDtypeStruct((channels // 4, 384, 256), BF16),
            jax.ShapeDtypeStruct((chunk * 24, chunk * 32), BF16),
        ),
        in_specs=[smem(), vmem()],
        out_specs=(vmem(), vmem(), vmem()),
        scratch_shapes=[pltpu.VMEM((beams, 256), F32)],
        cost_estimate=pl.CostEstimate(flops=10**6, bytes_accessed=2 * 10**6, transcendentals=0),
        name="prep",
    )(beam_index, beam_taps)


def smooth_group(group, index_ref, strips, col_ref, row_ref, hi_ref, mid_ref, sm_ref):
    columns = strips[0].shape[2]
    blocks = columns // 256
    tiles = columns // 128
    lane = lax.broadcasted_iota(jnp.int32, (128, 128), 1)

    def keep(tile, piece):
        hi, mid = split2(piece)
        for place in range(4):
            rows = slice(place * 32, place * 32 + 32)
            hi_ref[place, tile] = hi[rows]
            mid_ref[place, tile] = mid[rows]

    def row_step(n, tail):
        cols = pl.ds(pl.multiple_of(n * 256, 256), 256)
        data = jnp.concatenate(
            [ref[place, :, cols] for place in range(4) for ref in strips], axis=0
        )
        full = jnp.dot(row_ref[0], data, preferred_element_type=F32)
        value = full[0:128] + full[128:256] + full[256:384]
        moved = pltpu.roll(value, 64, 1)
        keep(2 * n, jnp.where(lane < 64, tail, moved[:, 0:128]))
        keep(2 * n + 1, moved[:, 128:256])
        return moved[:, 0:128]

    tail = lax.fori_loop(0, blocks, row_step, jnp.zeros((128, 128), F32), unroll=ROW_UNROLL)
    keep(tiles, jnp.where(lane < 64, tail, 0.0))

    def col_step(place, carry):
        channel = group * 4 + place
        band = col_ref[index_ref[channel]]
        rows = pl.ds(pl.multiple_of(channel * 32, 32), 32)
        for start in range(0, tiles, COL_RUN):
            total = None
            for ref in (hi_ref, mid_ref):
                data = jnp.concatenate(
                    [
                        ref[place, start : start + COL_RUN].reshape(COL_RUN * 32, 128),
                        ref[place, start + 1 : start + COL_RUN + 1].reshape(COL_RUN * 32, 128),
                    ],
                    axis=1,
                )
                term = lax.dot_general(data, band, NT, preferred_element_type=F32)
                total = term if total is None else total + term
            value = (total[:, 0:128] + total[:, 128:256]).astype(BF16)
            sm_ref[start : start + COL_RUN, rows, :] = value.reshape(COL_RUN, 32, 128)
        return carry

    lax.fori_loop(0, 4, col_step, 0, unroll=COL_UNROLL)


def place_tiles(sm_refs, order_ref, out_ref):
    channels = out_ref.shape[1]
    lane3 = lax.broadcasted_iota(jnp.int32, (12, channels, 128), 2)

    def place_step(n, carry):
        data = jnp.concatenate(
            [
                jnp.concatenate([ref[2 * n + t] for ref in sm_refs], axis=0)
                for t in range(2)
            ],
            axis=1,
        )
        moved = jnp.dot(order_ref[...], data, preferred_element_type=F32)
        for t in range(2):
            four = moved[:, t * 128 : t * 128 + 128].reshape(12, 2, channels, 128)
            even, odd = four[:, 0], four[:, 1]
            low = jnp.where(lane3 < 64, even, pltpu.roll(odd, 64, 2)).astype(BF16)
            high = jnp.where(lane3 < 64, pltpu.roll(even, 64, 2), odd).astype(BF16)
            for q in range(12):
                out_ref[4 * n + 2 * t, :, q * 128 : q * 128 + 128] = low[q]
                out_ref[4 * n + 2 * t + 1, :, q * 128 : q * 128 + 128] = high[q]
        return carry

    lax.fori_loop(0, out_ref.shape[0] // 4, place_step, 0, unroll=PLACE_UNROLL)


def smooth_kernel(
    index_ref, before, top, bottom, after, col_ref, row_ref, order_ref, out_ref, hi_ref, mid_ref, sm_ref
):
    group = pl.program_id(0)
    strips = (before, top, bottom, after)
    smooth_group(group, index_ref, strips, col_ref, row_ref, hi_ref, mid_ref, sm_ref)

    @pl.when(group == pl.num_programs(0) - 1)
    def _():
        place_tiles((sm_ref,), order_ref, out_ref)


def first_kernel(
    index_ref, before, top, bottom, after, col_ref, row_ref, sm_ref, hi_ref, mid_ref
):
    strips = (before, top, bottom, after)
    smooth_group(0, index_ref, strips, col_ref, row_ref, hi_ref, mid_ref, sm_ref)


def second_kernel(
    index_ref, before, top, bottom, after, col_ref, row_ref, first_ref, order_ref, out_ref, hi_ref, mid_ref, sm_ref
):
    strips = (before, top, bottom, after)
    smooth_group(0, index_ref, strips, col_ref, row_ref, hi_ref, mid_ref, sm_ref)
    place_tiles((first_ref, sm_ref), order_ref, out_ref)


def smooth_cost(channels):
    return pl.CostEstimate(
        flops=5 * 10**8 * channels, bytes_accessed=10**6 * channels, transcendentals=0
    )


def half_scratch(tiles):
    return [pltpu.VMEM((4, tiles + 1, 32, 128), BF16)] * 2


def smooth_first(beam_index, halo, col, row):
    tiles = halo[0].shape[2] // 128
    return pl.pallas_call(
        first_kernel,
        out_shape=jax.ShapeDtypeStruct((tiles, 128, 128), BF16),
        in_specs=[smem()] + [vmem()] * 6,
        out_specs=vmem(),
        scratch_shapes=half_scratch(tiles),
        compiler_params=pltpu.CompilerParams(vmem_limit_bytes=VMEM_LIMIT),
        cost_estimate=smooth_cost(4),
        name="first",
    )(beam_index, *halo, col, row)


def smooth_second(beam_index, halo, col, row, first, order):
    columns = halo[0].shape[2]
    tiles = columns // 128
    return pl.pallas_call(
        second_kernel,
        out_shape=jax.ShapeDtypeStruct((columns // 64, 8, 1536), BF16),
        in_specs=[smem()] + [vmem()] * 8,
        out_specs=vmem(),
        scratch_shapes=half_scratch(tiles) + [pltpu.VMEM((tiles, 128, 128), BF16)],
        compiler_params=pltpu.CompilerParams(vmem_limit_bytes=VMEM_LIMIT),
        cost_estimate=smooth_cost(4),
        name="second",
    )(beam_index, *halo, col, row, first, order)


def smooth(beam_index, before, top, bottom, after, col, row, order):
    channels, _, columns = before.shape
    tiles = columns // 128
    strip = pl.BlockSpec((4, 16, columns), lambda g: (g, 0, 0))
    return pl.pallas_call(
        smooth_kernel,
        grid=(channels // 4,),
        out_shape=jax.ShapeDtypeStruct((columns // 64, channels, 1536), BF16),
        in_specs=[smem()]
        + [strip] * 4
        + [
            pl.BlockSpec(col.shape, lambda g: (0, 0, 0)),
            pl.BlockSpec((1,) + row.shape[1:], lambda g: (g, 0, 0)),
            pl.BlockSpec(order.shape, lambda g: (0, 0)),
        ],
        out_specs=pl.BlockSpec((columns // 64, channels, 1536), lambda g: (0, 0, 0)),
        scratch_shapes=half_scratch(tiles) + [pltpu.VMEM((tiles, channels * 32, 128), BF16)],
        compiler_params=pltpu.CompilerParams(vmem_limit_bytes=VMEM_LIMIT),
        cost_estimate=smooth_cost(channels),
        name="smooth",
    )(beam_index, before, top, bottom, after, col, row, order)


def load_parts(parts, data_ref, sems):
    copies, first = [], 0
    for k, part in enumerate(parts):
        rows = part.shape[0]
        copies.append(
            pltpu.make_async_copy(part, data_ref.at[first : first + rows], sems.at[k])
        )
        first += rows
    for copy in copies:
        copy.start()
    return copies


def cov_kernel(core_ref, part0, part1, keep_ref, send_ref, tiles_ref, data_ref, sems, tiles_sem):
    for copy in load_parts((part0, part1, part0), data_ref, sems):
        copy.wait()
    tiles_copy = pltpu.make_async_copy(
        data_ref.at[0 : tiles_ref.shape[0]], tiles_ref, tiles_sem
    )
    tiles_copy.start()
    core = core_ref[0]

    def fill(out_ref, first):
        for unit in range(2):
            start = pl.multiple_of((first + 2 * unit) * 128, 256)
            wide = lax.dot_general(
                data_ref[pl.ds(start, 768), :],
                data_ref[pl.ds(start, 256), :],
                NT,
                preferred_element_type=F32,
            ).astype(out_ref.dtype)
            out_ref[2 * unit] = wide[0:640, 0:128]
            out_ref[2 * unit + 1] = wide[128:768, 128:256]

    fill(keep_ref, core * 4)
    fill(send_ref, (1 - core) * 4)
    tiles_copy.wait()


def anywhere():
    return pl.BlockSpec(memory_space=pl.ANY)


def local_covariance(core, parts):
    rows = sum(part.shape[0] for part in parts)
    return pl.pallas_call(
        cov_kernel,
        out_shape=(
            jax.ShapeDtypeStruct((4, 640, 128), F32),
            jax.ShapeDtypeStruct((4, 640, 128), BF16),
            jax.ShapeDtypeStruct((rows, parts[0].shape[1]), BF16),
        ),
        in_specs=[smem(), anywhere(), anywhere()],
        out_specs=(vmem(), vmem(), pl.BlockSpec(memory_space=pltpu.HBM)),
        scratch_shapes=[
            pltpu.VMEM((rows + parts[0].shape[0], parts[0].shape[1]), BF16),
            pltpu.SemaphoreType.DMA((3,)),
            pltpu.SemaphoreType.DMA,
        ],
        compiler_params=pltpu.CompilerParams(vmem_limit_bytes=VMEM_LIMIT),
        cost_estimate=pl.CostEstimate(
            flops=2 * 10**9, bytes_accessed=6 * 10**6, transcendentals=0
        ),
        name="cov",
    )(core, *parts)


def everywhere(x, axes, size):
    copies = jnp.broadcast_to(x[None], (size,) + x.shape)
    return lax.all_to_all(copies, axes, 0, 0, tiled=True)


def reduce_all(keep, send):
    swap = [(0, 1), (1, 0)]
    half = (keep + lax.ppermute(send, "core", swap).astype(F32)).astype(BF16)
    got = lax.all_to_all(half.reshape(4, 640, 128), "sky", 0, 0, tiled=True)
    quarter = jnp.sum(got.astype(F32), axis=0).astype(BF16)
    got = lax.all_to_all(quarter.reshape(32, 20, 128), ("y", "z"), 0, 0, tiled=True)
    mine = jnp.sum(got.astype(F32), axis=0)
    quarter = everywhere(mine, ("y", "z"), 32).reshape(640, 128)
    half = everywhere(quarter, "sky", 4).reshape(4, 640, 128)
    other = lax.ppermute(half, "core", swap)
    return half, other


def start_factor(gram):
    size = gram.shape[0]
    row = lax.broadcasted_iota(jnp.int32, (size, 128), 0)
    lane = lax.broadcasted_iota(jnp.int32, (size, 128), 1)
    unit = jnp.where(lane == row, 1.0, 0.0).astype(F32)
    columns = [jnp.broadcast_to(gram[:, j : j + 1], (size, 128)) for j in range(size)]
    return columns + [unit, jnp.ones((size, 128), F32)]


def eliminate(work, j):
    size = len(work) - 2
    shape = work[0].shape
    row = lax.broadcasted_iota(jnp.int32, shape, 0)
    pivot = jnp.broadcast_to(work[j][j : j + 1, :], shape)
    factor = jnp.where(row > j, work[j], 0.0) * (1.0 / pivot)
    new = list(work)
    for k in list(range(j + 1, size)) + [size]:
        new[k] = work[k] - factor * jnp.broadcast_to(work[k][j : j + 1, :], shape)
    new[size + 1] = jnp.where(row == j, pivot, work[size + 1])
    return new


def end_factor(work):
    inverse, pivot = work[-2], work[-1]
    size = inverse.shape[0]
    scale = lax.rsqrt(pivot)
    scale = scale * (1.5 - 0.5 * pivot * scale * scale)
    return (inverse * scale)[:, 0:size]


def clean_kernel(
    core_ref, near_ref, far_ref, seed_ref, tiles_ref, out_ref, data_ref, cov_ref, basis_ref, coef_ref, done_ref, sem, out_sems
):
    core = core_ref[0]
    tiles_copy = pltpu.make_async_copy(tiles_ref, data_ref, sem)
    tiles_copy.start()
    modes = seed_ref.shape[0] // 3
    count = seed_ref.shape[1]
    pixels = data_ref.shape[1]
    scale = 1.0 / (256 * pixels)
    for i in range(8):
        for d in range(5):
            rows = slice(d * 128, d * 128 + 128)
            near, far = near_ref[i % 4, rows, :], far_ref[i % 4, rows, :]
            block = jnp.where(core == i // 4, near, far) * scale
            j = (i + d) % 8
            hi, mid = split2(block)
            cov_ref[j * 128 : j * 128 + 128, i * 256 : i * 256 + 128] = hi
            cov_ref[j * 128 : j * 128 + 128, i * 256 + 128 : i * 256 + 256] = mid
            if d in (1, 2, 3):
                hi, mid = split2(block.T)
                cov_ref[i * 128 : i * 128 + 128, j * 256 : j * 256 + 128] = hi
                cov_ref[i * 128 : i * 128 + 128, j * 256 + 128 : j * 256 + 256] = mid

    def fold(x):
        return x[0:modes] + x[modes : 2 * modes] + x[2 * modes : 3 * modes]

    def stack(x):
        return jnp.concatenate(split3(x), axis=0)

    def cov_block(parts, q):
        wide = fold(
            jnp.dot(parts, cov_ref[:, q * 256 : q * 256 + 256], preferred_element_type=F32)
        )
        return wide[:, 0:128] + wide[:, 128:256]

    def gram_of(parts):
        tall = fold(lax.dot_general(parts, parts, NT, preferred_element_type=F32))
        return tall[:, 0:modes] + tall[:, modes : 2 * modes] + tall[:, 2 * modes : 3 * modes]

    def exact_dot(a, b):
        return lax.dot(a, b, precision=lax.Precision.HIGHEST, preferred_element_type=F32)

    seeds = seed_ref[...]
    images = jnp.concatenate([cov_block(seeds, q) for q in range(8)], axis=1)

    def sweep(step, images):
        parts = stack(images)
        work = start_factor(gram_of(parts))
        blocks = []
        for q in range(8):
            blocks.append(cov_block(parts, q))
            work = eliminate(eliminate(work, 2 * q), 2 * q + 1)
        return exact_dot(end_factor(work), jnp.concatenate(blocks, axis=1))

    images = lax.fori_loop(0, ITERS - 1, sweep, images)
    work = start_factor(gram_of(stack(images)))
    for j in range(modes):
        work = eliminate(work, j)
    basis = exact_dot(end_factor(work), images)
    hi, mid, low = split3(basis)
    basis_ref[...] = jnp.concatenate([hi, hi, mid, mid, hi, low], axis=0)
    tiles_copy.wait()
    data = data_ref[...]
    coef = fold(
        jnp.dot(jnp.concatenate([hi, mid, low], axis=0), data, preferred_element_type=F32)
    )
    hi, mid, low = split3(coef)
    coef_ref[...] = jnp.concatenate([hi, mid, hi, mid, low, hi], axis=0)
    sent = []
    for m in range(count // 128):
        rows = slice(m * 128, m * 128 + 128)
        part = lax.dot_general(
            basis_ref[:, rows], coef_ref[...], TN, preferred_element_type=F32
        )
        value = (data_ref[rows, :].astype(F32) - part).astype(BF16)
        chunk, first = m // 4, (m % 4) * 16
        done_ref[m] = value.reshape(16, 8, pixels)
        copy = pltpu.make_async_copy(
            done_ref.at[m],
            out_ref.at[first : first + 16, chunk * 8 : chunk * 8 + 8, :],
            out_sems.at[m],
        )
        copy.start()
        sent.append(copy)
    for copy in sent:
        copy.wait()


def seeds_kernel(seed_ref, out_ref):
    out_ref[...] = jnp.concatenate(split3(seed_ref[...].astype(F32)), axis=0)


def split_seed(seed):
    modes, count = seed.shape
    return pl.pallas_call(
        seeds_kernel,
        out_shape=jax.ShapeDtypeStruct((3 * modes, count), BF16),
        in_specs=[vmem()],
        out_specs=vmem(),
        name="seeds",
    )(seed)


def clean(core, near, far, seed, tiles):
    modes, count = seed.shape
    modes = modes // 3
    pixels = tiles.shape[1]
    return pl.pallas_call(
        clean_kernel,
        out_shape=jax.ShapeDtypeStruct((count // 16, 16, pixels), BF16),
        in_specs=[smem()] + [vmem()] * 3 + [pl.BlockSpec(memory_space=pltpu.HBM)],
        out_specs=anywhere(),
        scratch_shapes=[
            pltpu.VMEM((count, pixels), BF16),
            pltpu.VMEM((count, 2 * count), BF16),
            pltpu.VMEM((6 * modes, count), BF16),
            pltpu.VMEM((6 * modes, pixels), BF16),
            pltpu.VMEM((count // 128, 16, 8, pixels), BF16),
            pltpu.SemaphoreType.DMA,
            pltpu.SemaphoreType.DMA((count // 128,)),
        ],
        compiler_params=pltpu.CompilerParams(vmem_limit_bytes=VMEM_LIMIT),
        cost_estimate=pl.CostEstimate(
            flops=3 * 10**9, bytes_accessed=12 * 10**6, transcendentals=0
        ),
        name="clean",
    )(core, near, far, seed, tiles)


def body(sky_maps, beam_index, beam_taps, start_seed):
    channels, strip_rows, _ = sky_maps.shape
    modes = start_seed.shape[1]
    core = lax.axis_index("core").astype(jnp.int32).reshape(1)
    col, row, order = prepare(beam_index, beam_taps, CHUNK)
    halos = []
    for first, last in ((0, 4), (4, 8), (8, 16)):
        strip = sky_maps if first == 0 else lax.optimization_barrier(sky_maps)
        strip = strip[first:last]
        top = strip[:, 0:16, :]
        bottom = strip[:, strip_rows - 16 : strip_rows, :]
        before = lax.ppermute(bottom, "sky", [(i, i + 1) for i in range(3)])
        after = lax.ppermute(top, "sky", [(i + 1, i) for i in range(3)])
        halos.append((before, top, bottom, after))
    first = smooth_first(beam_index[0:4], halos[0], col, row[0:1])
    pieces0 = smooth_second(beam_index[4:8], halos[1], col, row[1:2], first, order)
    pieces1 = smooth(beam_index[8:16], *halos[2], col, row[2:4], order)
    parts = []
    for pieces in (pieces0, pieces1):
        data = lax.all_to_all(pieces, ("y", "z", "core"), 0, 0, tiled=True)
        parts.append(data.reshape(64 * CHUNK, 1536))
    seed = start_seed.T.reshape(modes, 64, channels // CHUNK, CHUNK)
    seed = seed.transpose(0, 2, 1, 3).reshape(modes, 64 * channels)
    seed = split_seed(seed)
    keep, send, tiles = local_covariance(core, parts)
    near, far = reduce_all(keep, send)
    cleaned = clean(core, near, far, seed, tiles)
    return cleaned.reshape(64 * channels, 1, 1536)


def solution(mesh):
    fine = Mesh(mesh.devices.reshape(4, 8, 2, 4), ("y", "z", "core", "sky"))
    freq = ("y", "z", "core")

    return jax.shard_map(
        body,
        mesh=fine,
        in_specs=(P(freq, "sky", None), P(freq), P(), P()),
        out_specs=P(None, freq + ("sky",), None),
        check_vma=False,
    )
```
